256 devices in a mesh: ctx: 64 (over z, x, core), head: 4 (over y).
Axes of the slice: x: 4, y: 4, z: 8, core: 2. Of those that a mesh axis runs over, the one named last changes fastest.
Arguments:
- queries: bfloat16 [32768, 2048], P('ctx', 'head'), may hold values from -6 to 6
- keys: bfloat16 [32768, 2048], P('ctx', 'head'), may hold values from -6 to 6
- values: bfloat16 [32768, 2048], P('ctx', 'head'), may hold values from -6 to 6
- out_grad: bfloat16 [32768, 2048], P('ctx', 'head'), may hold values from -6 to 6
- inputs: bfloat16 [32768, 4096], P('ctx', 'head'), may hold values from -16 to 16
- value_weight: bfloat16 [4096, 2048], P('ctx', 'head'), may hold values from -0.25 to 0.25
Outputs:
- query_grad: bfloat16 [32768, 2048], P('ctx', 'head')
- key_grad: bfloat16 [32768, 2048], P('ctx', 'head')
- input_grad: bfloat16 [32768, 4096], P('ctx', 'head')
- weight_grad: float32 [4096, 2048], P('ctx', 'head')
The draws below stay inside these ranges and needn't reach their ends.
All inputs are finite; a program needn't handle non-finite values.
Results may differ from the reference program's by a relative error of at most 0.0049.
Values may be sent and summed in bfloat16 or wider, within the bound.
A program may use at most 128 MiB of HBM per device.

```python
import math
import jax
import jax.numpy as jnp
from jax import lax

D = 4096
HEADS = 16
DH = 128
TOK_DEV = 512
TOKENS = 32768
HD = 2048


def with_spikes(entries, stream_key, source, target, shards_of, factor):
    owner, partner = [(jnp.arange(entries.shape[position]) // (entries.shape[position] // shards_of)).reshape([-1 if axis == position else 1 for axis in range(entries.ndim)]) for position in (source, target)]
    chosen = jax.random.permutation(stream_key, shards_of)[partner]
    strong = (owner == chosen) | (owner == (partner + shards_of // 2) % shards_of)
    return jnp.where(strong, factor * entries, entries)


def block_scale(own_key, dims, pieces, low, high):
    loudness = 1.0
    for axis_at, parts in pieces:
        steps = jax.random.uniform(jax.random.fold_in(jax.random.fold_in(own_key, 6), axis_at), (parts,), jnp.float32, low / len(pieces), high / len(pieces))
        loudness = loudness * jnp.repeat(jnp.exp(steps), dims[axis_at] // parts).reshape((-1,) + (1,) * (len(dims) - 1 - axis_at))
    return loudness


def bell_draw(rng, shape, width, limit, cuts=(), dtype=jnp.bfloat16):
    factor_of = block_scale(rng, shape, cuts, -0.22, 0.18) if cuts else 1.0
    drawn = jax.random.normal(rng, shape, jnp.float32) * width * factor_of
    return jnp.minimum(jnp.maximum(drawn, -limit), limit).astype(dtype)


def noise_with(rng, shape, deviation, bound, shards, heavy, dtype=jnp.bfloat16):
    values = deviation * jax.random.normal(rng, shape, jnp.float32)
    if shards:
        values = values * block_scale(rng, shape, shards, -0.22, 0.18)
    return jnp.clip(with_spikes(values, jax.random.fold_in(rng, 3), *heavy), -bound, bound).astype(dtype)


def setup_inputs(seed: int = 0) -> dict:
    splits = jax.random.split(jax.random.key(seed), 7)
    queries = bell_draw(splits[0], (TOKENS, HD), 1.0, 6.0, ((0, 64), (1, 4)))
    keys = bell_draw(splits[1], (TOKENS, HD), 1.0, 6.0, ((0, 64), (1, 4)))
    values = bell_draw(splits[2], (TOKENS, HD), 1.0, 6.0, ((0, 64), (1, 4)))
    out_grad = bell_draw(splits[3], (TOKENS, HD), 1.0, 6.0, ((0, 64), (1, 4)))
    inputs = noise_with(splits[4], (TOKENS, D), 1.0, 16.0, ((0, 64), (1, 4)), (0, 1, 64, 4.0))
    value_weight = noise_with(splits[5], (D, HD), D ** -0.5, 0.25, ((0, 64), (1, 4)), (1, 0, 64, 4.0))
    return dict(queries=queries, keys=keys, values=values, out_grad=out_grad, inputs=inputs, value_weight=value_weight)


def reference(queries, keys, values, out_grad, inputs, value_weight):
    blocks = TOKENS // TOK_DEV
    factor = 1.0 / math.sqrt(DH * TOKENS)
    highest = lax.Precision.HIGHEST

    def split(array):
        return array.astype(jnp.float32).reshape(blocks, TOK_DEV, HEADS, DH)
    query_all = split(queries)
    key_all = split(keys)
    value_all = split(values)
    grad_all = split(out_grad)
    kv_state = jnp.einsum('bthd,bthe->bhde', key_all, value_all, precision=highest)
    qg_state = jnp.einsum('bthd,bthe->bhde', query_all, grad_all, precision=highest)
    prior = jnp.cumsum(kv_state, axis=0) - kv_state
    later = jnp.cumsum(qg_state[::-1], axis=0)[::-1] - qg_state
    rows = lax.broadcasted_iota(jnp.int32, (TOK_DEV, TOK_DEV), 0)
    cols = lax.broadcasted_iota(jnp.int32, (TOK_DEV, TOK_DEV), 1)
    causal = rows >= cols

    def rounded(array):
        return lax.optimization_barrier(array.astype(jnp.bfloat16)).astype(jnp.float32)

    def one_block(item):
        query_blk, key_blk, value_blk, grad_blk, prior_blk, later_blk = item
        grad_scores = rounded(jnp.where(causal[None], jnp.einsum('the,she->hts', grad_blk, value_blk, precision=highest), 0.0))
        key_scores = rounded(jnp.where(causal[None], jnp.einsum('thd,shd->hts', query_blk, key_blk, precision=highest), 0.0))
        query_out = factor * (jnp.einsum('the,hde->thd', grad_blk, prior_blk, precision=highest) + jnp.einsum('hts,shd->thd', grad_scores, key_blk, precision=highest))
        key_out = factor * (jnp.einsum('hts,thd->shd', grad_scores, query_blk, precision=highest) + jnp.einsum('she,hde->shd', value_blk, later_blk, precision=highest))
        value_out = factor * (jnp.einsum('hts,the->she', key_scores, grad_blk, precision=highest) + jnp.einsum('shd,hde->she', key_blk, later_blk, precision=highest))
        return (query_out.astype(jnp.bfloat16), key_out.astype(jnp.bfloat16), value_out.astype(jnp.bfloat16))
    query_out, key_out, value_out = lax.map(one_block, (query_all, key_all, value_all, grad_all, prior, later))
    query_grad = query_out.reshape(TOKENS, HD)
    key_grad = key_out.reshape(TOKENS, HD)
    value_grad = value_out.reshape(TOKENS, HD)
    input_grad = jnp.dot(value_grad, value_weight.T, preferred_element_type=jnp.float32).astype(jnp.bfloat16)
    weight_grad = jnp.dot(inputs.T, value_grad, preferred_element_type=jnp.float32) * (1.0 / math.sqrt(TOKENS))
    return (query_grad, key_grad, input_grad, weight_grad)
```

```python
import functools
import math

import jax
import jax.numpy as jnp
from jax import lax
from jax.experimental import pallas as pl
from jax.experimental.pallas import tpu as pltpu
from jax.sharding import PartitionSpec as P

DH = 128
NX, NZ, NC, NY = 4, 8, 2, 4
F32, BF16 = jnp.float32, jnp.bfloat16
MESH = pl.DeviceIdType.MESH
NT = (((1,), (1,)), ((), ()))
NN = (((1,), (0,)), ((), ()))


def mm(a, b, dims=NN):
    return lax.dot_general(a, b, dims, preferred_element_type=F32)


def kernel(
    factor, wscale,
    q_hbm, k_hbm, v_hbm, g_hbm, in_hbm, w_hbm,
    q_out, k_out, i_out, w_out,
    qh, kh, vh, gh, inb, int_, wz, wbuf,
    sq, sk, r1q, r1k, wsq, wsk, t2q, t2k, z2q, z2k, zaq, zak, o3q, o3k, later, prior,
    qloc, kloc, vloc, vgall, vsib, part, acc,
    sxa, sxb, sxc, rxa, rxb, rxc, yrecv, ysend, zrecv,
    lsem, ssem, p1sem, p2sem, p3sem, w1sem, w2sem, w3sem, w4sem, isem, ysem, svsem, xsem, ymsem, zsem,
):
    c, h = lax.axis_index("ctx"), lax.axis_index("head")
    z, m = c // 8, c % 8
    x, kk = m // 2, m % 2

    def cidx(zz, xx, cc):
        return zz * 8 + xx * 2 + cc

    sib = cidx(z, x, 1 - kk)
    xr, xl = (x + 1) % NX, (x + 3) % NX
    yr, yl, yo = (h + 1) % NY, (h + 3) % NY, (h + 2) % NY

    pending = []
    count = [0]

    def send(src, dst, rsem, ctx, head, cond=None):
        desc = pltpu.make_async_remote_copy(
            src_ref=src, dst_ref=dst, send_sem=ssem.at[count[0]], recv_sem=rsem,
            device_id=(ctx, head), device_id_type=MESH)
        count[0] += 1
        if cond is None:
            desc.start()
        else:
            pl.when(cond)(desc.start)
        pending.append((cond, desc))

    def arrived(dst, sem, cond=None):
        desc = pltpu.make_async_copy(dst, dst, sem)
        if cond is None:
            desc.wait()
        else:
            pl.when(cond)(desc.wait)

    loads = {}
    n = 0
    for j in range(4):
        for name, src, dst in (("q", q_hbm, qh), ("g", g_hbm, gh)):
            loads[name, j] = pltpu.make_async_copy(src.at[:, pl.ds(DH * j, DH)], dst.at[j], lsem.at[n])
            n += 1
    for j in range(4):
        for name, src, dst in (("k", k_hbm, kh), ("v", v_hbm, vh)):
            loads[name, j] = pltpu.make_async_copy(src.at[:, pl.ds(DH * j, DH)], dst.at[j], lsem.at[n])
            n += 1
    loads["w"] = pltpu.make_async_copy(w_hbm, wz.at[z], lsem.at[n])
    loads["i"] = pltpu.make_async_copy(in_hbm, inb.at[0], lsem.at[n + 1])
    for desc in loads.values():
        desc.start()

    barrier = pltpu.get_barrier_semaphore()
    partners = 0

    def greet(ctx, head):
        pl.semaphore_signal(barrier, inc=1, device_id=(ctx, head), device_id_type=MESH)

    for off in range(1, 8):
        mm_ = (m + off) % 8
        greet(z * 8 + mm_, h)
        partners += 1
    for off in range(1, 8):
        zz = (z + off) % NZ
        for cc in range(NC):
            greet(cidx(zz, x, cc), h)
            partners += 1
    for off in range(1, 4):
        greet(c, (h + off) % NY)
        partners += 1

    for j in range(4):
        loads["q", j].wait()
        loads["g", j].wait()
        sq[j] = mm(qh[j].T, gh[j]).astype(BF16)
    pl.semaphore_wait(barrier, partners)

    def scan1(s, r1, row):
        for off in range(1, 8):
            to = (m + off) % 8
            send(s.at[to // 2, pl.ds(pl.multiple_of(64 * (to % 2), 64), 64)], r1.at[m],
                 p1sem.at[row, off], z * 8 + to, h)
        r1[m] = s[x, pl.ds(pl.multiple_of(64 * kk, 64), 64), :]

    def scan2(r1, ws, t2, z2, row, reverse):
        for off in range(1, 8):
            arrived(r1.at[(m + 8 - off) % 8], p1sem.at[row, off])
        total = jnp.zeros((64, DH), F32)
        order = range(7, -1, -1) if reverse else range(8)
        for i in order:
            ws[i] = total
            total = total + r1[i].astype(F32)
        t2[...] = total
        for d in range(1, NZ):
            zz = z - d if reverse else z + d
            cond = zz >= 0 if reverse else zz < NZ
            send(t2, z2.at[d], p2sem.at[row, d], cidx(jnp.clip(zz, 0, NZ - 1), x, kk), h, cond)

    def scan3(ws, z2, za, o3, full, row, reverse):
        za[...] = jnp.zeros((64, DH), F32)
        for d in range(1, NZ):
            cond = z + d < NZ if reverse else z - d >= 0

            @pl.when(cond)
            def _():
                arrived(z2.at[d], p2sem.at[row, d])
                za[...] += z2[d]
        for i in range(8):
            o3[i] = (ws[i] + za[...]).astype(BF16)
        for off in range(1, 8):
            to = (m + off) % 8
            send(o3.at[to], full.at[x, pl.ds(pl.multiple_of(64 * kk, 64), 64)],
                 p3sem.at[row, off], z * 8 + to, h)
        full[x, pl.ds(pl.multiple_of(64 * kk, 64), 64), :] = o3[m]

    def scan_done(full, row):
        for off in range(1, 8):
            at = (m + 8 - off) % 8
            arrived(full.at[at // 2, pl.ds(pl.multiple_of(64 * (at % 2), 64), 64)], p3sem.at[row, off])

    scan1(sq, r1q, 0)

    loads["w"].wait()
    for off in range(1, NZ):
        send(wz.at[z], wz.at[z], w1sem, cidx((z + off) % NZ, x, kk), h)
    loads["i"].wait()
    send(inb.at[0], inb.at[1], isem, sib, h)

    for j in range(4):
        loads["k", j].wait()
        loads["v", j].wait()
        sk[j] = mm(kh[j].T, vh[j]).astype(BF16)
    scan1(sk, r1k, 1)

    def masked_t(a, b, width):
        s = mm(a, b, NT)
        rows = lax.broadcasted_iota(jnp.int32, (256, width), 0)
        cols = lax.broadcasted_iota(jnp.int32, (256, width), 1)
        return jnp.where(rows <= cols, s, 0.0).astype(BF16)

    def transposed_part(a, b, c_, out):
        def step(j, carry):
            for i in range(2):
                lo = 256 * i
                s = masked_t(a[j, lo:lo + 256, :], b[j, lo:512, :], 512 - lo)
                out[j, lo:lo + 256, :] = mm(s, c_[j, lo:512, :])
            return carry
        lax.fori_loop(0, 4, step, 0)

    def straight_part(a, b, c_, out):
        def step(j, carry):
            for i in range(2):
                lo, hi = 256 * i, 256 * i + 256
                s = mm(a[j, lo:hi, :], b[j, 0:hi, :], NT)
                rows = lax.broadcasted_iota(jnp.int32, (256, hi), 0) + lo
                cols = lax.broadcasted_iota(jnp.int32, (256, hi), 1)
                s = jnp.where(rows >= cols, s, 0.0).astype(BF16)
                out[j, lo:hi, :] = mm(s, c_[j, 0:hi, :])
            return carry
        lax.fori_loop(0, 4, step, 0)

    scan2(r1q, wsq, t2q, z2q, 0, True)
    transposed_part(kh, qh, gh, vloc)
    scan2(r1k, wsk, t2k, z2k, 1, False)

    def transpose_inputs(slot):
        def step(j, carry):
            at = pl.multiple_of(128 * j, 128)
            int_[slot, pl.ds(at, 128), :] = inb[slot, :, pl.ds(at, 128)].T
            return carry
        lax.fori_loop(0, 8, step, 0)

    transpose_inputs(0)
    scan3(wsq, z2q, zaq, o3q, later, 0, True)

    arrived(wz.at[pl.ds(0, 7)], w1sem)
    for off in range(1, NY):
        to = (h + off) % NY
        send(wz.at[pl.ds(2 * to, 2)], wbuf.at[h, :, x, kk], w2sem.at[off], c, to)
    wbuf[h, 0, x, kk] = wz[2 * h]
    wbuf[h, 1, x, kk] = wz[2 * h + 1]

    scan3(wsk, z2k, zak, o3k, prior, 1, False)
    arrived(inb.at[1], isem)

    scan_done(later, 0)
    for cc in range(2):
        for j in (2 * cc, 2 * cc + 1):
            val = factor * (vloc[j] + mm(kh[j], later[j]))
            vgall[h, cc, :, pl.ds(128 * (j % 2), 128)] = val.astype(BF16)
        send(vgall.at[h, cc], vgall.at[h, cc], ysem.at[0, cc], c, yr)
        send(vgall.at[h, cc], vgall.at[h, cc], ysem.at[1, cc], c, yl)
    send(vgall.at[h, 1 - kk], vsib.at[0], svsem.at[0], sib, h)

    for off in range(1, NY):
        arrived(wbuf.at[(h + NY - off) % NY, :, x, kk], w2sem.at[off])
    for b in range(2):
        send(wbuf.at[:, b, x, kk], wbuf.at[:, b, x, kk], w3sem.at[0, b], cidx(z, xr, kk), h)
        send(wbuf.at[:, b, x, kk], wbuf.at[:, b, x, kk], w3sem.at[1, b], cidx(z, xl, kk), h)
    send(wbuf.at[:, :, x, kk], wbuf.at[:, :, x, kk], w4sem.at[0], sib, h)

    transpose_inputs(1)

    origins = (h, yl, yr, yo)
    movers = (h, yl, yr, yo)
    senders = (h, yr, yl, yo)

    def partial(e):
        def step(i, carry):
            rows = pl.ds(pl.multiple_of(256 * i, 256), 256)
            p = mm(int_[0, rows, :], vgall[origins[e], kk]) + mm(int_[1, rows, :], vsib[e])
            b, x0 = i // 2, 2 * (i % 2)
            part[e, x0, b] = p[:128]
            part[e, x0 + 1, b] = p[128:]
            return carry
        lax.fori_loop(0, 4, step, 0)

    def ways(e):
        return (xr, xl) if e % 2 == 0 else (xl, xr)

    def xsend1(e):
        fw, bw = ways(e)
        sxa[e] = part[e, (x + 2) % NX].astype(BF16)
        send(sxa.at[e], rxa.at[e], xsem.at[0, e], cidx(z, fw, kk), h)
        sxb[e] = part[e, bw].astype(BF16)
        send(sxb.at[e], rxb.at[e], xsem.at[1, e], cidx(z, bw, kk), h)

    def xsend2(e):
        fw, bw = ways(e)
        arrived(rxa.at[e], xsem.at[0, e])
        sxc[e] = (part[e, fw] + rxa[e].astype(F32)).astype(BF16)
        send(sxc.at[e], rxc.at[e], xsem.at[2, e], cidx(z, fw, kk), h)

    def zsend(s):
        for b in range(2):
            for kr in range(2):
                to = cidx(2 * senders[s] + b, x, kr)
                send(yrecv.at[s, b, pl.ds(64 * kr, 64)], zrecv.at[z * 2 + kk], zsem, to, h, to != c)

                @pl.when(to == c)
                def _():
                    zrecv[z * 2 + kk] = yrecv[s, b, 64 * kr:64 * kr + 64, :]

    def xdone(e):
        arrived(rxb.at[e], xsem.at[1, e])
        arrived(rxc.at[e], xsem.at[2, e])
        total = part[e, x] + rxb[e].astype(F32) + rxc[e].astype(F32)
        if e == 0:
            yrecv[0] = total.astype(BF16)
            zsend(0)
        else:
            ysend[e] = total.astype(BF16)
            send(ysend.at[e], yrecv.at[e], ymsem.at[e], c, movers[e])

    def ydone(s):
        arrived(yrecv.at[s], ymsem.at[s])
        zsend(s)

    def input_part(e, first):
        o = origins[e]

        def step(i, carry):
            b, x0 = i // 2, 2 * (i % 2)
            w = wbuf[o, b, pl.ds(x0, 2)].reshape(256, 512)
            p = mm(vgall[o, 0], w[:, :256], NT) + mm(vgall[o, 1], w[:, 256:], NT)
            acc[i] = p if first else acc[i] + p
            return carry
        lax.fori_loop(0, 4, step, 0)

    arrived(vsib.at[0], svsem.at[0])
    partial(0)
    xsend1(0)
    transposed_part(vh, gh, qh, kloc)
    xsend2(0)

    def key_step(j, carry):
        at = pl.ds(pl.multiple_of(128 * j, 128), 128)
        k_out[:, at] = (factor * (kloc[j] + mm(vh[j], later[j], NT))).astype(BF16)
        return carry
    lax.fori_loop(0, 4, key_step, 0)

    for b in range(2):
        arrived(wbuf.at[:, b, xl, kk], w3sem.at[0, b])
        if b == 0:
            send(wbuf.at[:, 0, xl, kk], wbuf.at[:, 0, xl, kk], w3sem.at[2, 0], cidx(z, xr, kk), h)
    for b in (1, 0):
        arrived(wbuf.at[:, b, xr, kk], w3sem.at[1, b])
        if b == 1:
            send(wbuf.at[:, 1, xr, kk], wbuf.at[:, 1, xr, kk], w3sem.at[2, 1], cidx(z, xl, kk), h)
    send(wbuf.at[:, :, xl, kk], wbuf.at[:, :, xl, kk], w4sem.at[1], sib, h)
    send(wbuf.at[:, :, xr, kk], wbuf.at[:, :, xr, kk], w4sem.at[2], sib, h)
    xdone(0)

    straight_part(gh, vh, kh, qloc)
    scan_done(prior, 1)

    def query_step(j, carry):
        at = pl.ds(pl.multiple_of(128 * j, 128), 128)
        q_out[:, at] = (factor * (qloc[j] + mm(gh[j], prior[j], NT))).astype(BF16)
        return carry
    lax.fori_loop(0, 4, query_step, 0)

    arrived(vgall.at[yl, 0], ysem.at[0, 0])
    send(vgall.at[yl, 0], vgall.at[yl, 0], ysem.at[2, 0], c, yr)
    arrived(vgall.at[yr, 0], ysem.at[1, 0])
    arrived(vgall.at[yr, 1], ysem.at[1, 1])
    send(vgall.at[yr, 1], vgall.at[yr, 1], ysem.at[2, 1], c, yl)
    arrived(vgall.at[yl, 1], ysem.at[0, 1])
    send(vgall.at[yl, 1 - kk], vsib.at[1], svsem.at[1], sib, h)
    send(vgall.at[yr, 1 - kk], vsib.at[2], svsem.at[2], sib, h)
    arrived(vsib.at[1], svsem.at[1])
    partial(1)
    xsend1(1)
    arrived(vsib.at[2], svsem.at[2])
    partial(2)
    xsend1(2)
    xsend2(1)
    xsend2(2)
    for b in range(2):
        arrived(wbuf.at[:, b, (x + 2) % NX, kk], w3sem.at[2, b])
    send(wbuf.at[:, :, (x + 2) % NX, kk], wbuf.at[:, :, (x + 2) % NX, kk], w4sem.at[3], sib, h)
    xdone(1)
    xdone(2)
    for i, at in enumerate((x, xl, xr, (x + 2) % NX)):
        arrived(wbuf.at[:, :, at, 1 - kk], w4sem.at[i])
    input_part(0, True)
    ydone(1)
    ydone(2)

    arrived(vgall.at[yo, 0], ysem.at[2, 0])
    arrived(vgall.at[yo, 1], ysem.at[2, 1])
    send(vgall.at[yo, 1 - kk], vsib.at[3], svsem.at[3], sib, h)
    arrived(vsib.at[3], svsem.at[3])
    partial(3)
    xsend1(3)
    input_part(1, False)
    xsend2(3)
    input_part(2, False)
    xdone(3)
    input_part(3, False)
    ydone(3)
    for i in range(4):
        i_out[:, 256 * i:256 * i + 256] = acc[i].astype(BF16)

    arrived(zrecv.at[pl.ds(0, 15)], zsem)
    for cc in range(2):
        total = zrecv[cc].astype(F32)
        for zz in range(1, NZ):
            total = total + zrecv[2 * zz + cc].astype(F32)
        w_out[:, 256 * cc:256 * cc + 256] = total * wscale

    for cond, desc in pending:
        if cond is None:
            desc.wait_send()
        else:
            pl.when(cond)(desc.wait_send)


def local(queries, keys, values, out_grad, inputs, value_weight):
    length = queries.shape[0]
    tokens = length * lax.axis_size("ctx")
    factor = 1.0 / math.sqrt(DH * tokens)
    wscale = 1.0 / math.sqrt(tokens)
    vm = pltpu.VMEM
    dma = pltpu.SemaphoreType.DMA
    scratch = [
        vm((4, 512, 128), BF16), vm((4, 512, 128), BF16), vm((4, 512, 128), BF16), vm((4, 512, 128), BF16),
        vm((2, 512, 1024), BF16), vm((2, 1024, 512), BF16),
        vm((8, 64, 512), BF16), vm((4, 2, 4, 2, 64, 512), BF16),
        vm((4, 128, 128), BF16), vm((4, 128, 128), BF16),
        vm((8, 64, 128), BF16), vm((8, 64, 128), BF16),
        vm((8, 64, 128), F32), vm((8, 64, 128), F32),
        vm((64, 128), F32), vm((64, 128), F32),
        vm((8, 64, 128), F32), vm((8, 64, 128), F32),
        vm((64, 128), F32), vm((64, 128), F32),
        vm((8, 64, 128), BF16), vm((8, 64, 128), BF16),
        vm((4, 128, 128), BF16), vm((4, 128, 128), BF16),
        vm((4, 512, 128), F32), vm((4, 512, 128), F32), vm((4, 512, 128), F32),
        vm((4, 2, 512, 256), BF16), vm((4, 512, 256), BF16),
        vm((4, 4, 2, 128, 256), F32), vm((4, 512, 256), F32),
        vm((4, 2, 128, 256), BF16), vm((4, 2, 128, 256), BF16), vm((4, 2, 128, 256), BF16),
        vm((4, 2, 128, 256), BF16), vm((4, 2, 128, 256), BF16), vm((4, 2, 128, 256), BF16),
        vm((4, 2, 128, 256), BF16), vm((4, 2, 128, 256), BF16),
        vm((16, 64, 256), BF16),
        dma((18,)), dma((128,)), dma((2, 8)), dma((2, 8)), dma((2, 8)),
        dma(()), dma((4,)), dma((3, 2)), dma((4,)), dma(()), dma((3, 2)), dma((4,)), dma((3, 4)), dma((4,)), dma(()),
    ]
    out_shape = (
        jax.ShapeDtypeStruct((512, 512), BF16),
        jax.ShapeDtypeStruct((512, 512), BF16),
        jax.ShapeDtypeStruct((512, 1024), BF16),
        jax.ShapeDtypeStruct((64, 512), F32),
    )
    return pl.pallas_call(
        functools.partial(kernel, factor, wscale),
        out_shape=out_shape,
        in_specs=[pl.BlockSpec(memory_space=pl.ANY)] * 6,
        out_specs=[pl.BlockSpec(memory_space=pltpu.VMEM)] * 4,
        scratch_shapes=scratch,
        compiler_params=pltpu.CompilerParams(
            collective_id=0, has_side_effects=True, vmem_limit_bytes=56 * 1024 * 1024),
        name="attention_backward",
    )(queries, keys, values, out_grad, inputs, value_weight)


def solution(mesh):
    spec = P("ctx", "head")
    return jax.shard_map(
        local, mesh=mesh, in_specs=(spec,) * 6, out_specs=(spec,) * 4, check_vma=False)
```

```python
import functools
import math

import jax
import jax.numpy as jnp
from jax import lax
from jax.experimental import pallas as pl
from jax.experimental.pallas import tpu as pltpu
from jax.sharding import PartitionSpec as P

DH = 128
NX, NZ, NC, NY = 4, 8, 2, 4
F32, BF16 = jnp.float32, jnp.bfloat16
MESH = pl.DeviceIdType.MESH
NT = (((1,), (1,)), ((), ()))
NN = (((1,), (0,)), ((), ()))


def mm(a, b, dims=NN):
    return lax.dot_general(a, b, dims, preferred_element_type=F32)


def kernel(
    factor, wscale,
    q_hbm, k_hbm, v_hbm, g_hbm, in_hbm, w_hbm,
    q_out, k_out, i_out, w_out,
    qh, kh, vh, gh, inb, int_, wz, wbuf,
    sq, sk, r1q, r1k, wsq, wsk, t2q, t2k, z2q, z2k, zaq, zak, o3q, o3k, later, prior,
    qloc, kloc, vloc, vgall, vsib, part, acc,
    sxa, sxb, sxc, rxa, rxb, rxc, zs, zr, zfs, zfr, xfs, xfr, fs, fr, qs, ks, ist,
    lsem, ssem, p1sem, p2sem, p3sem, w1sem, w2sem, w3sem, w4sem, isem, ysem, svsem, xsem, zsem, fsem, osem,
):
    c, h = lax.axis_index("ctx"), lax.axis_index("head")
    z, m = c // 8, c % 8
    x, kk = m // 2, m % 2

    def cidx(zz, xx, cc):
        return zz * 8 + xx * 2 + cc

    sib = cidx(z, x, 1 - kk)
    xr, xl = (x + 1) % NX, (x + 3) % NX
    yr, yl, yo = (h + 1) % NY, (h + 3) % NY, (h + 2) % NY

    pending = []
    count = [0]

    def group(n=1):
        count[0] += n
        return ssem.at[count[0] - n] if n == 1 else [ssem.at[count[0] - n + i] for i in range(n)]

    def send(src, dst, rsem, ctx, head, sem, cond=None):
        desc = pltpu.make_async_remote_copy(
            src_ref=src, dst_ref=dst, send_sem=sem, recv_sem=rsem,
            device_id=(ctx, head), device_id_type=MESH)
        if cond is None:
            desc.start()
        else:
            pl.when(cond)(desc.start)
        return desc

    def sent(ref, sem):
        pending.append((None, pltpu.make_async_copy(ref, ref, sem)))

    def arrived(dst, sem, cond=None):
        desc = pltpu.make_async_copy(dst, dst, sem)
        if cond is None:
            desc.wait()
        else:
            pl.when(cond)(desc.wait)

    for n, (src, dst) in enumerate(((q_hbm, qh), (g_hbm, gh), (k_hbm, kh), (v_hbm, vh))):
        for j in range(4):
            pltpu.make_async_copy(src.at[:, pl.ds(DH * j, DH)], dst.at[j], lsem.at[n]).start()
    load_w = pltpu.make_async_copy(w_hbm, wz.at[z], lsem.at[4])
    load_w.start()
    load_i = pltpu.make_async_copy(in_hbm, inb.at[0], lsem.at[5])
    load_i.start()

    barrier = pltpu.get_barrier_semaphore()
    partners = 0

    def greet(ctx, head):
        pl.semaphore_signal(barrier, inc=1, device_id=(ctx, head), device_id_type=MESH)

    for off in range(1, 8):
        mm_ = (m + off) % 8
        greet(z * 8 + mm_, h)
        partners += 1
    for off in range(1, 8):
        zz = (z + off) % NZ
        greet(cidx(zz, x, kk), h)
        partners += 1
    for off in range(1, 4):
        greet(c, (h + off) % NY)
        partners += 1

    arrived(qh, lsem.at[0])
    arrived(gh, lsem.at[1])
    for j in range(4):
        sq[j] = mm(qh[j].T, gh[j])
    arrived(kh, lsem.at[2])
    arrived(vh, lsem.at[3])
    for j in range(4):
        sk[j] = mm(kh[j].T, vh[j])
    pl.semaphore_wait(barrier, partners)

    def scan1(s, r1, row):
        sem = group()
        for off in range(1, 8):
            to = (m + off) % 8
            send(s.at[to // 2, pl.ds(pl.multiple_of(64 * (to % 2), 64), 64)], r1.at[m],
                 p1sem.at[row], z * 8 + to, h, sem)
        sent(r1.at[pl.ds(0, 7)], sem)
        r1[m] = s[x, pl.ds(pl.multiple_of(64 * kk, 64), 64), :]

    def scan2(r1, ws, t2, z2, row, reverse):
        arrived(r1.at[pl.ds(0, 7)], p1sem.at[row])
        total = jnp.zeros((64, DH), F32)
        order = range(7, -1, -1) if reverse else range(8)
        for i in order:
            ws[i] = total
            total = total + r1[i]
        t2[...] = total.astype(BF16)
        for d in range(1, NZ):
            zz = z - d if reverse else z + d
            cond = zz >= 0 if reverse else zz < NZ
            desc = send(t2, z2.at[d], p2sem.at[row, d], cidx(jnp.clip(zz, 0, NZ - 1), x, kk), h, group(), cond)
            pending.append((cond, desc))

    def scan3(ws, z2, za, o3, full, row, reverse):
        za[...] = jnp.zeros((64, DH), F32)
        for d in range(1, NZ):
            cond = z + d < NZ if reverse else z - d >= 0

            @pl.when(cond)
            def _():
                arrived(z2.at[d], p2sem.at[row, d])
                za[...] += z2[d].astype(F32)
        for i in range(8):
            o3[i] = (ws[i] + za[...]).astype(BF16)
        sem = group()
        for off in range(1, 8):
            to = (m + off) % 8
            send(o3.at[to], full.at[x, pl.ds(pl.multiple_of(64 * kk, 64), 64)],
                 p3sem.at[row], z * 8 + to, h, sem)
        sent(o3.at[pl.ds(0, 7)], sem)
        full[x, pl.ds(pl.multiple_of(64 * kk, 64), 64), :] = o3[m]

    def scan_done(o3, row):
        arrived(o3.at[pl.ds(0, 7)], p3sem.at[row])

    scan1(sq, r1q, 0)

    wnsem, wzsem = group(), group()

    def wnext(zs):
        to = zs // 2
        send(wz.at[zs], wbuf.at[h, zs % 2, x, kk], w2sem, c, to, wnsem, to != h)

        @pl.when(to == h)
        def _():
            wbuf[h, zs % 2, x, kk] = wz[zs]

    def wz_to(at, sem, dz):
        send(wz.at[at], wz.at[at], sem, cidx((z + dz + NZ) % NZ, x, kk), h, wzsem)

    def wring1():
        load_w.wait()
        for d in (1, 2):
            wz_to(z, w1sem.at[0, d], d)
            wz_to(z, w1sem.at[1, d], -d)
        wnext(z)

    def wring2():
        right, left = (z + 6) % NZ, (z + 2) % NZ
        arrived(wz.at[right], w1sem.at[0, 2])
        arrived(wz.at[left], w1sem.at[1, 2])
        wz_to(right, w1sem.at[0, 3], 1)
        wz_to(left, w1sem.at[1, 3], -1)
        wz_to(right, w1sem.at[0, 4], 2)
        wnext(right)
        wnext(left)
        for side, at in ((0, (z + 7) % NZ), (1, (z + 1) % NZ)):
            arrived(wz.at[at], w1sem.at[side, 1])
            wnext(at)

    def wring3():
        for side, d, at in ((0, 3, (z + 5) % NZ), (1, 3, (z + 3) % NZ), (0, 4, (z + 4) % NZ)):
            arrived(wz.at[at], w1sem.at[side, d])
            wnext(at)

    wring1()
    scan1(sk, r1k, 1)
    load_i.wait()
    insem = group()
    send(inb.at[0], inb.at[1], isem, sib, h, insem)
    sent(inb.at[0], insem)

    def masked_t(a, b, width):
        s = mm(a, b, NT)
        rows = lax.broadcasted_iota(jnp.int32, (256, width), 0)
        cols = lax.broadcasted_iota(jnp.int32, (256, width), 1)
        return jnp.where(rows <= cols, s, 0.0).astype(BF16)

    def transposed_part(a, b, c_, out):
        def step(j, carry):
            for i in range(2):
                lo = 256 * i
                s = masked_t(a[j, lo:lo + 256, :], b[j, lo:512, :], 512 - lo)
                out[j, lo:lo + 256, :] = mm(s, c_[j, lo:512, :])
            return carry
        lax.fori_loop(0, 4, step, 0)

    def straight_part(a, b, c_, out):
        def step(j, carry):
            for i in range(2):
                lo, hi = 256 * i, 256 * i + 256
                s = mm(a[j, lo:hi, :], b[j, 0:hi, :], NT)
                rows = lax.broadcasted_iota(jnp.int32, (256, hi), 0) + lo
                cols = lax.broadcasted_iota(jnp.int32, (256, hi), 1)
                s = jnp.where(rows >= cols, s, 0.0).astype(BF16)
                out[j, lo:hi, :] = mm(s, c_[j, 0:hi, :])
            return carry
        lax.fori_loop(0, 4, step, 0)

    def transpose_inputs(slot):
        def step(j, carry):
            at = pl.multiple_of(128 * j, 128)
            int_[slot, pl.ds(at, 128), :] = inb[slot, :, pl.ds(at, 128)].T
            return carry
        lax.fori_loop(0, 8, step, 0)

    sent(wz.at[pl.ds(0, 6)], wnsem)
    sent(wz.at[pl.ds(0, 7)], wzsem)
    scan2(r1q, wsq, t2q, z2q, 0, True)
    wring2()
    transposed_part(kh, qh, gh, vloc)
    scan2(r1k, wsk, t2k, z2k, 1, False)
    transpose_inputs(0)
    arrived(inb.at[1], isem)
    transpose_inputs(1)
    scan3(wsq, z2q, zaq, o3q, later, 0, True)
    wring3()
    scan3(wsk, z2k, zak, o3k, prior, 1, False)

    scan_done(o3q, 0)
    for j in range(4):
        val = factor * (vloc[j] + mm(kh[j], later[j]))
        vgall[h, j] = val.astype(BF16)
    ygsem, yrsem, fwsem = group(), group(), group()
    for j in range(4):
        send(vgall.at[h, j], vgall.at[h, j], ysem.at[0, j], c, yr, ygsem)
        jj = (j + 2) % 4
        send(vgall.at[h, jj], vgall.at[h, jj], ysem.at[1, jj], c, yl, ygsem)
    send(vgall.at[h, pl.ds(2 * (1 - kk), 2)], vsib.at[0], svsem.at[0], sib, h, fwsem)
    sent(vgall.at[pl.ds(0, 2)], ygsem)
    sent(vgall.at[0], yrsem)
    sent(vgall.at[pl.ds(0, 2)], fwsem)

    def pick(first, second):
        return jnp.where(kk == 0, first, second)

    origins = (h, pick(yl, yr), pick(yr, yl), yo, yo)
    sib_origins = (h, origins[2], origins[1], yo, yo)
    heads = ((0, 1), (0, 1), (0, 1), (0,), (1,))
    cols = tuple(128 * len(js) for js in heads)

    def forward(e):
        js = heads[e]
        send(vgall.at[sib_origins[e], pl.ds(2 * (1 - kk) + js[0], len(js))], vsib.at[e, pl.ds(0, len(js))],
             svsem.at[e], sib, h, fwsem)

    def pair(ref, at, j, n):
        if n == 1:
            return ref[at, j]
        return jnp.concatenate([ref[at, j], ref[at, j + 1]], axis=1)

    def partial(e):
        w = cols[e]

        def own(i, carry):
            rows = pl.ds(pl.multiple_of(256 * i, 256), 256)
            p = mm(int_[0, rows, :], pair(vgall, origins[e], 2 * kk + heads[e][0], len(heads[e])))
            b, x0 = i // 2, 2 * (i % 2)
            part[e, x0, b, :, :w] = p[:128]
            part[e, x0 + 1, b, :, :w] = p[128:]
            return carry

        def other(i, carry):
            rows = pl.ds(pl.multiple_of(256 * i, 256), 256)
            p = mm(int_[1, rows, :], pair(vsib, e, 0, len(heads[e])))
            b, x0 = i // 2, 2 * (i % 2)
            part[e, x0, b, :, :w] += p[:128]
            part[e, x0 + 1, b, :, :w] += p[128:]
            return carry

        lax.fori_loop(0, 4, own, 0)
        arrived(vsib.at[e, pl.ds(0, len(heads[e]))], svsem.at[e])
        lax.fori_loop(0, 4, other, 0)

    def ways(e):
        return (xr, xl) if e == 2 else (xl, xr)

    xgsem, zgsem, fgsem, zfsem, xfsem = group(), group(), group(), group(2), group(2)

    def cut(ref, e):
        return ref.at[e, :, :, pl.ds(0, cols[e])]

    def xsend1(e):
        fw, bw = ways(e)
        w = cols[e]
        sxa[e, :, :, :w] = part[e, (x + 2) % NX, :, :, :w].astype(BF16)
        send(cut(sxa, e), cut(rxa, e), xsem.at[0, e], cidx(z, fw, kk), h, xgsem)
        sxb[e, :, :, :w] = part[e, bw, :, :, :w].astype(BF16)
        send(cut(sxb, e), cut(rxb, e), xsem.at[1, e], cidx(z, bw, kk), h, xgsem)

    def xsend2(e):
        fw, bw = ways(e)
        w = cols[e]
        arrived(cut(rxa, e), xsem.at[0, e])
        sxc[e, :, :, :w] = (part[e, fw, :, :, :w] + rxa[e, :, :, :w].astype(F32)).astype(BF16)
        send(cut(sxc, e), cut(rxc, e), xsem.at[2, e], cidx(z, fw, kk), h, xgsem)

    def xdone(e):
        w = cols[e]
        arrived(cut(rxb, e), xsem.at[1, e])
        arrived(cut(rxc, e), xsem.at[2, e])
        for p in range(NZ):
            b, r0 = p % 2, 64 * (p // 2 % 2) + 32 * (p // 4)
            total = (part[e, x, b, r0:r0 + 32, :w] + rxb[e, b, r0:r0 + 32, :w].astype(F32)
                     + rxc[e, b, r0:r0 + 32, :w].astype(F32))
            zs[e, p, :, :w] = total.astype(BF16)
        for dz in range(1, NZ):
            to = (z + dz) % NZ
            send(zs.at[e, to, :, pl.ds(0, w)], zr.at[e, z, :, pl.ds(0, w)], zsem.at[e], cidx(to, x, kk), h, zgsem)
        zr[e, z, :, :w] = zs[e, z, :, :w]

    mine = (h == z // 2) & (kk == z // 2 % 2)
    slot = 2 * kk + z // 4

    def finish(e, total):
        w = cols[e]
        lo = 128 if e == 4 else 0
        fs[e, :, :w] = total * wscale
        to = cidx(2 * h + z % 2, x, z // 2 % 2)
        if e == 0:
            other = jnp.logical_not(mine)
            pending.append((other, send(fs.at[0], fr.at[slot], fsem, to, h, group(), other)))

            @pl.when(mine)
            def _():
                fr[slot] = fs[0]
        else:
            send(fs.at[e, :, pl.ds(0, w)], fr.at[slot, :, pl.ds(lo, w)], fsem, to, origins[e], fgsem)

    def zdone(e):
        w = cols[e]
        arrived(zr.at[e, pl.ds(0, 7), :, pl.ds(0, w)], zsem.at[e])
        total = zr[e, 0, :, :w].astype(F32)
        for zz in range(1, NZ):
            total = total + zr[e, zz, :, :w].astype(F32)
        finish(e, total)

    def zfirst(e):
        for p in range(NZ):
            b, r0 = p % 2, 64 * (p // 2 % 2) + 32 * (p // 4)
            zfs[e, p] = part[e, :, b, r0:r0 + 32, :].astype(BF16)
        for dz in range(1, NZ):
            to = (z + dz) % NZ
            send(zfs.at[e, to], zfr.at[e, z], zsem.at[e], cidx(to, x, kk), h, zfsem[e])
        zfr[e, z] = zfs[e, z]
        sent(zfr.at[e, pl.ds(0, 7)], zfsem[e])

    def xnext(e):
        arrived(zfr.at[e, pl.ds(0, 7)], zsem.at[e])
        for xx in range(NX):
            total = zfr[e, 0, xx].astype(F32)
            for zz in range(1, NZ):
                total = total + zfr[e, zz, xx].astype(F32)
            xfs[e, xx] = total.astype(BF16)
        for dx in range(1, NX):
            to = (x + dx) % NX
            send(xfs.at[e, to], xfr.at[e, x], xsem.at[0, e], cidx(z, to, kk), h, xfsem[e])
        xfr[e, x] = xfs[e, x]
        sent(xfr.at[e, pl.ds(0, 3)], xfsem[e])

    def xlast(e):
        arrived(xfr.at[e, pl.ds(0, 3)], xsem.at[0, e])
        total = xfr[e, 0].astype(F32)
        for xx in range(1, NX):
            total = total + xfr[e, xx].astype(F32)
        finish(e, total)

    def key_step(j, carry):
        at = pl.ds(pl.multiple_of(128 * j, 128), 128)
        ks[:, at] = (factor * (kloc[j] + mm(vh[j], later[j], NT))).astype(BF16)
        return carry

    def query_step(j, carry):
        at = pl.ds(pl.multiple_of(128 * j, 128), 128)
        qs[:, at] = (factor * (qloc[j] + mm(gh[j], prior[j], NT))).astype(BF16)
        return carry

    def put(src, dst, n):
        pltpu.make_async_copy(src, dst, osem.at[n]).start()

    xo = (x + 2) % NX

    def wblock(u, b, at):
        return wbuf.at[(h + u) % NY, b, at, kk]

    wxsem, wrsem, wssem = group(), group(), group()

    def wx(u):
        for b in range(2):
            send(wblock(u, b, x), wblock(u, b, x), w3sem.at[2 * b, u], cidx(z, xr, kk), h, wxsem)
            send(wblock(u, 1 - b, x), wblock(u, 1 - b, x), w3sem.at[1 + b, u], cidx(z, xl, kk), h, wxsem)

    def wrelay(u):
        arrived(wblock(u, 0, xl), w3sem.at[0, u])
        send(wblock(u, 0, xl), wblock(u, 0, xl), w3sem.at[3, u], cidx(z, xr, kk), h, wrsem)
        arrived(wblock(u, 1, xr), w3sem.at[1, u])
        send(wblock(u, 1, xr), wblock(u, 1, xr), w3sem.at[3, u], cidx(z, xl, kk), h, wrsem)

    def wsib(u, n):
        ref = wbuf.at[(h + u) % NY, :, (x, xl, xr, xo)[n], kk]
        send(ref, ref, w4sem.at[u], sib, h, wssem)

    def wneighbours(u):
        arrived(wbuf.at[(h + u) % NY, :, xl, kk], w3sem.at[2, u])
        wsib(u, 1)
        wsib(u, 2)

    def wopposite(u):
        arrived(wbuf.at[(h + u) % NY, :, xo, kk], w3sem.at[3, u])
        wsib(u, 3)

    def input_part(u):
        o = (h + u) % NY
        arrived(wbuf.at[o, :, :, 1 - kk], w4sem.at[u])

        def step(i, carry):
            b, x0 = i // 2, 2 * (i % 2)
            w = wbuf[o, b, pl.ds(x0, 2)].reshape(256, 512)
            p = mm(pair(vgall, o, 0, 2), w[:, :256], NT) + mm(pair(vgall, o, 2, 2), w[:, 256:], NT)
            if u == 3:
                ist[i] = (acc[i] + p).astype(BF16)
            else:
                acc[i] = p if u == 0 else acc[i] + p
            return carry
        lax.fori_loop(0, 4, step, 0)

    partial(0)
    zfirst(0)
    arrived(wz.at[pl.ds(0, 6)], w2sem)
    for u in range(NY):
        wx(u)
    for u in range(NY):
        wsib(u, 0)
    transposed_part(vh, gh, qh, kloc)
    lax.fori_loop(0, 4, key_step, 0)
    put(ks, k_out, 0)

    for j in range(2):
        arrived(vgall.at[yl, j], ysem.at[0, j])
        send(vgall.at[yl, j], vgall.at[yl, j], ysem.at[2, j], c, yr, yrsem)
        arrived(vgall.at[yr, 2 + j], ysem.at[1, 2 + j])
        send(vgall.at[yr, 2 + j], vgall.at[yr, 2 + j], ysem.at[2, 2 + j], c, yl, yrsem)
    forward(1)
    partial(1)
    zfirst(1)
    straight_part(gh, vh, kh, qloc)
    scan_done(o3k, 1)
    lax.fori_loop(0, 4, query_step, 0)
    put(qs, q_out, 0)
    wrelay(0)
    wrelay(1)

    for j in range(2):
        arrived(vgall.at[yl, 2 + j], ysem.at[0, 2 + j])
        arrived(vgall.at[yr, j], ysem.at[1, j])
    forward(2)
    partial(2)
    xsend1(2)
    wrelay(2)
    wrelay(3)
    xnext(0)
    wneighbours(0)
    wneighbours(1)

    for j in (0, 2):
        arrived(vgall.at[yo, j], ysem.at[2, j])
    forward(3)
    partial(3)
    xsend1(3)
    xsend2(2)
    for j in (1, 3):
        arrived(vgall.at[yo, j], ysem.at[2, j])
    forward(4)
    partial(4)
    xsend1(4)
    xlast(0)
    wneighbours(2)
    wneighbours(3)
    xdone(2)
    xsend2(3)
    xsend2(4)
    xnext(1)
    wopposite(0)
    wopposite(1)
    input_part(0)
    xdone(3)
    xdone(4)
    wopposite(2)
    wopposite(3)
    xlast(1)
    input_part(1)
    zdone(2)
    input_part(2)
    zdone(3)
    zdone(4)
    input_part(3)
    for i in range(4):
        put(ist.at[i], i_out.at[:, pl.ds(256 * i, 256)], 1)
    sent(vgall.at[pl.ds(0, 2)], wxsem)
    sent(vgall.at[0], wrsem)
    sent(vgall, wssem)
    sent(vsib.at[pl.ds(0, 3)], xgsem)
    sent(zs.at[pl.ds(0, 2), pl.ds(0, 7)], zgsem)
    sent(fr.at[pl.ds(0, 3)], fgsem)

    @pl.when(mine)
    def _():
        arrived(fr.at[pl.ds(0, 3)], fsem)

    @pl.when(jnp.logical_not(mine))
    def _():
        arrived(fr, fsem)

    for n in range(4):
        put(fr.at[n], w_out.at[pl.ds(32 * (n % 2), 32), pl.ds(256 * (n // 2), 256)], 2)
    arrived(vgall.at[pl.ds(0, 2)], osem.at[0])
    arrived(ist, osem.at[1])
    arrived(fr, osem.at[2])
    for cond, desc in pending:
        if cond is None:
            desc.wait()
        else:
            pl.when(cond)(desc.wait_send)


def write_out(q_in, k_in, i_in, w_in, q_out, k_out, i_out, w_out, sems):
    pairs = ((i_in, i_out), (q_in, q_out), (k_in, k_out), (w_in, w_out))
    copies = [pltpu.make_async_copy(src, dst, sems.at[n]) for n, (src, dst) in enumerate(pairs)]
    for copy in copies:
        copy.start()
    for copy in copies:
        copy.wait()


def local(queries, keys, values, out_grad, inputs, value_weight):
    length = queries.shape[0]
    tokens = length * lax.axis_size("ctx")
    factor = 1.0 / math.sqrt(DH * tokens)
    wscale = 1.0 / math.sqrt(tokens)
    vm = pltpu.VMEM
    dma = pltpu.SemaphoreType.DMA
    scratch = [
        vm((4, 512, 128), BF16), vm((4, 512, 128), BF16), vm((4, 512, 128), BF16), vm((4, 512, 128), BF16),
        vm((2, 512, 1024), BF16), vm((2, 1024, 512), BF16),
        vm((8, 64, 512), BF16), vm((4, 2, 4, 2, 64, 512), BF16),
        vm((4, 128, 128), F32), vm((4, 128, 128), F32),
        vm((8, 64, 128), F32), vm((8, 64, 128), F32),
        vm((8, 64, 128), F32), vm((8, 64, 128), F32),
        vm((64, 128), BF16), vm((64, 128), BF16),
        vm((8, 64, 128), BF16), vm((8, 64, 128), BF16),
        vm((64, 128), F32), vm((64, 128), F32),
        vm((8, 64, 128), BF16), vm((8, 64, 128), BF16),
        vm((4, 128, 128), BF16), vm((4, 128, 128), BF16),
        vm((4, 512, 128), F32), vm((4, 512, 128), F32), vm((4, 512, 128), F32),
        vm((4, 4, 512, 128), BF16), vm((5, 2, 512, 128), BF16),
        vm((5, 4, 2, 128, 256), F32), vm((4, 512, 256), F32),
        vm((5, 2, 128, 256), BF16), vm((5, 2, 128, 256), BF16), vm((5, 2, 128, 256), BF16),
        vm((5, 2, 128, 256), BF16), vm((5, 2, 128, 256), BF16), vm((5, 2, 128, 256), BF16),
        vm((5, 8, 32, 256), BF16), vm((5, 8, 32, 256), BF16),
        vm((2, 8, 4, 32, 256), BF16), vm((2, 8, 4, 32, 256), BF16), vm((2, 4, 32, 256), BF16), vm((2, 4, 32, 256), BF16),
        vm((5, 32, 256), F32), vm((4, 32, 256), F32),
        vm((512, 512), BF16), vm((512, 512), BF16), vm((4, 512, 256), BF16),
        dma((6,)), dma((40,)), dma((2,)), dma((2, 8)), dma((2,)),
        dma((2, 5)), dma(()), dma((4, 4)), dma((4,)), dma(()), dma((3, 4)), dma((5,)), dma((3, 5)),
        dma((5,)), dma(()), dma((3,)),
    ]
    out_shape = (
        pltpu.VMEM((512, 512), BF16),
        pltpu.VMEM((512, 512), BF16),
        pltpu.VMEM((512, 1024), BF16),
        pltpu.VMEM((64, 512), F32),
    )
    results = pl.pallas_call(
        functools.partial(kernel, factor, wscale),
        out_shape=out_shape,
        in_specs=[pl.BlockSpec(memory_space=pl.ANY)] * 6,
        out_specs=[pl.BlockSpec(memory_space=pl.ANY)] * 4,
        scratch_shapes=scratch,
        compiler_params=pltpu.CompilerParams(
            collective_id=0, has_side_effects=True, vmem_limit_bytes=56 * 1024 * 1024),
        name="attention_backward",
    )(queries, keys, values, out_grad, inputs, value_weight)
    return pl.pallas_call(
        write_out,
        out_shape=tuple(jax.ShapeDtypeStruct(r.shape, r.dtype) for r in results),
        in_specs=[pl.BlockSpec(memory_space=pltpu.VMEM)] * 4,
        out_specs=[pl.BlockSpec(memory_space=pl.ANY)] * 4,
        scratch_shapes=[dma((4,))],
        name="write_out",
    )(*(pltpu.with_memory_space_constraint(r, pltpu.VMEM) for r in results))


def solution(mesh):
    spec = P("ctx", "head")
    return jax.shard_map(
        local, mesh=mesh, in_specs=(spec,) * 6, out_specs=(spec,) * 4, check_vma=False)
```

```python
import functools
import math

import jax
import jax.numpy as jnp
from jax import lax
from jax.experimental import pallas as pl
from jax.experimental.pallas import tpu as pltpu
from jax.sharding import PartitionSpec as P

DH = 128
NX, NZ, NC, NY = 4, 8, 2, 4
F32, BF16 = jnp.float32, jnp.bfloat16
MESH = pl.DeviceIdType.MESH
NT = (((1,), (1,)), ((), ()))
NN = (((1,), (0,)), ((), ()))


def mm(a, b, dims=NN):
    return lax.dot_general(a, b, dims, preferred_element_type=F32)


def kernel(
    factor, wscale,
    q_hbm, k_hbm, v_hbm, g_hbm, in_hbm, w_hbm,
    q_out, k_out, i_out, w_out,
    qh, kh, vh, gh, inb, int_, wz, wbuf,
    sq, sk, r1q, r1k, wsq, wsk, t2q, t2k, z2q, z2k, zaq, zak, o3q, o3k, later, prior,
    qloc, kloc, vloc, vgall, vsib, part, acc,
    sxa, sxb, sxc, rxa, rxb, rxc, zs, zr, zfs, zfr, xfs, xfr, fs, fr, qs, ks, ist,
    lsem, ssem, p1sem, p2sem, p3sem, w1sem, w2sem, w3sem, w4sem, isem, ysem, svsem, xsem, zsem, fsem, osem,
):
    c, h = lax.axis_index("ctx"), lax.axis_index("head")
    z, m = c // 8, c % 8
    x, kk = m // 2, m % 2

    def cidx(zz, xx, cc):
        return zz * 8 + xx * 2 + cc

    sib = cidx(z, x, 1 - kk)
    xr, xl = (x + 1) % NX, (x + 3) % NX
    yr, yl, yo = (h + 1) % NY, (h + 3) % NY, (h + 2) % NY

    pending = []
    count = [0]

    def group(n=1):
        count[0] += n
        return ssem.at[count[0] - n] if n == 1 else [ssem.at[count[0] - n + i] for i in range(n)]

    def send(src, dst, rsem, ctx, head, sem, cond=None):
        desc = pltpu.make_async_remote_copy(
            src_ref=src, dst_ref=dst, send_sem=sem, recv_sem=rsem,
            device_id=(ctx, head), device_id_type=MESH)
        if cond is None:
            desc.start()
        else:
            pl.when(cond)(desc.start)
        return desc

    def sent(ref, sem):
        pending.append((None, pltpu.make_async_copy(ref, ref, sem)))

    def arrived(dst, sem, cond=None):
        desc = pltpu.make_async_copy(dst, dst, sem)
        if cond is None:
            desc.wait()
        else:
            pl.when(cond)(desc.wait)

    for n, (src, dst) in enumerate(((q_hbm, qh), (g_hbm, gh), (k_hbm, kh), (v_hbm, vh))):
        for j in range(4):
            pltpu.make_async_copy(src.at[:, pl.ds(DH * j, DH)], dst.at[j], lsem.at[n]).start()
    load_w = pltpu.make_async_copy(w_hbm, wz.at[z], lsem.at[4])
    load_w.start()
    load_i = pltpu.make_async_copy(in_hbm, inb.at[0], lsem.at[5])
    load_i.start()

    barrier = pltpu.get_barrier_semaphore()
    partners = 0

    def greet(ctx, head):
        pl.semaphore_signal(barrier, inc=1, device_id=(ctx, head), device_id_type=MESH)

    for off in range(1, 8):
        mm_ = (m + off) % 8
        greet(z * 8 + mm_, h)
        partners += 1
    for off in range(1, 8):
        zz = (z + off) % NZ
        greet(cidx(zz, x, kk), h)
        partners += 1
    for off in range(1, 4):
        greet(c, (h + off) % NY)
        partners += 1

    arrived(qh, lsem.at[0])
    arrived(gh, lsem.at[1])
    for j in range(4):
        sq[j] = mm(qh[j].T, gh[j])
    arrived(kh, lsem.at[2])
    arrived(vh, lsem.at[3])
    for j in range(4):
        sk[j] = mm(kh[j].T, vh[j])
    pl.semaphore_wait(barrier, partners)

    plane = [2 * ((x + dx) % NX) + (kk + dk) % 2 for dx, dk in
             ((2, 0), (2, 1), (1, 0), (3, 0), (1, 1), (3, 1), (0, 1))]

    def scan1(s, r1, row):
        sem = group()
        for to in plane:
            send(s.at[to // 2, pl.ds(pl.multiple_of(64 * (to % 2), 64), 64)], r1.at[m],
                 p1sem.at[row], z * 8 + to, h, sem)
        sent(r1.at[pl.ds(0, 7)], sem)
        r1[m] = s[x, pl.ds(pl.multiple_of(64 * kk, 64), 64), :]

    def scan2(r1, ws, t2, z2, row, reverse):
        arrived(r1.at[pl.ds(0, 7)], p1sem.at[row])
        total = jnp.zeros((64, DH), F32)
        order = range(7, -1, -1) if reverse else range(8)
        for i in order:
            ws[i] = total
            total = total + r1[i]
        t2[...] = total.astype(BF16)
        for d in (4, 3, 5, 2, 6, 1, 7):
            zz = z - d if reverse else z + d
            cond = zz >= 0 if reverse else zz < NZ
            desc = send(t2, z2.at[d], p2sem.at[row, d], cidx(jnp.clip(zz, 0, NZ - 1), x, kk), h, group(), cond)
            pending.append((cond, desc))

    def scan3(ws, z2, za, o3, full, row, reverse):
        za[...] = jnp.zeros((64, DH), F32)
        for d in range(1, NZ):
            cond = z + d < NZ if reverse else z - d >= 0

            @pl.when(cond)
            def _():
                arrived(z2.at[d], p2sem.at[row, d])
                za[...] += z2[d].astype(F32)
        for i in range(8):
            o3[i] = (ws[i] + za[...]).astype(BF16)
        sem = group()
        for to in plane:
            send(o3.at[to], full.at[x, pl.ds(pl.multiple_of(64 * kk, 64), 64)],
                 p3sem.at[row], z * 8 + to, h, sem)
        sent(o3.at[pl.ds(0, 7)], sem)
        full[x, pl.ds(pl.multiple_of(64 * kk, 64), 64), :] = o3[m]

    def scan_done(o3, row):
        arrived(o3.at[pl.ds(0, 7)], p3sem.at[row])

    scan1(sq, r1q, 0)

    wnsem, wzsem = group(), group()

    def wnext(zs):
        to = zs // 2
        send(wz.at[zs], wbuf.at[h, zs % 2, x, kk], w2sem, c, to, wnsem, to != h)

        @pl.when(to == h)
        def _():
            wbuf[h, zs % 2, x, kk] = wz[zs]

    def wz_to(at, sem, dz):
        send(wz.at[at], wz.at[at], sem, cidx((z + dz + NZ) % NZ, x, kk), h, wzsem)

    def wring1():
        load_w.wait()
        for d in (2, 1):
            wz_to(z, w1sem.at[0, d], d)
            wz_to(z, w1sem.at[1, d], -d)
        wnext(z)

    def wring2():
        right, left = (z + 6) % NZ, (z + 2) % NZ
        arrived(wz.at[right], w1sem.at[0, 2])
        arrived(wz.at[left], w1sem.at[1, 2])
        wz_to(right, w1sem.at[0, 3], 1)
        wz_to(left, w1sem.at[1, 3], -1)
        wz_to(right, w1sem.at[0, 4], 2)
        wnext(right)
        wnext(left)

    def wring2b():
        for side, at in ((0, (z + 7) % NZ), (1, (z + 1) % NZ)):
            arrived(wz.at[at], w1sem.at[side, 1])
            wnext(at)

    def wring3():
        for side, d, at in ((0, 3, (z + 5) % NZ), (1, 3, (z + 3) % NZ), (0, 4, (z + 4) % NZ)):
            arrived(wz.at[at], w1sem.at[side, d])
            wnext(at)

    wring1()
    scan1(sk, r1k, 1)
    load_i.wait()
    insem = group()
    send(inb.at[0], inb.at[1], isem, sib, h, insem)
    sent(inb.at[0], insem)

    def masked_t(a, b, width):
        s = mm(a, b, NT)
        rows = lax.broadcasted_iota(jnp.int32, (256, width), 0)
        cols = lax.broadcasted_iota(jnp.int32, (256, width), 1)
        return jnp.where(rows <= cols, s, 0.0).astype(BF16)

    def transposed_part(a, b, c_, out):
        def step(j, carry):
            for i in range(2):
                lo = 256 * i
                s = masked_t(a[j, lo:lo + 256, :], b[j, lo:512, :], 512 - lo)
                out[j, lo:lo + 256, :] = mm(s, c_[j, lo:512, :])
            return carry
        lax.fori_loop(0, 4, step, 0)

    def straight_part(a, b, c_, out):
        def step(j, carry):
            for i in range(2):
                lo, hi = 256 * i, 256 * i + 256
                s = mm(a[j, lo:hi, :], b[j, 0:hi, :], NT)
                rows = lax.broadcasted_iota(jnp.int32, (256, hi), 0) + lo
                cols = lax.broadcasted_iota(jnp.int32, (256, hi), 1)
                s = jnp.where(rows >= cols, s, 0.0).astype(BF16)
                out[j, lo:hi, :] = mm(s, c_[j, 0:hi, :])
            return carry
        lax.fori_loop(0, 4, step, 0)

    def transpose_inputs(slot):
        def step(j, carry):
            at = pl.multiple_of(128 * j, 128)
            int_[slot, pl.ds(at, 128), :] = inb[slot, :, pl.ds(at, 128)].T
            return carry
        lax.fori_loop(0, 8, step, 0)

    sent(wz.at[pl.ds(0, 6)], wnsem)
    sent(wz.at[pl.ds(0, 7)], wzsem)
    scan2(r1q, wsq, t2q, z2q, 0, True)
    wring2()
    transposed_part(kh, qh, gh, vloc)
    wring2b()
    scan2(r1k, wsk, t2k, z2k, 1, False)
    transpose_inputs(0)
    arrived(inb.at[1], isem)
    transpose_inputs(1)
    scan3(wsq, z2q, zaq, o3q, later, 0, True)
    wring3()

    scan_done(o3q, 0)
    for j in range(4):
        val = factor * (vloc[j] + mm(kh[j], later[j]))
        vgall[h, j] = val.astype(BF16)
    ygsem, yrsem, fwsem = group(), group(), group()
    for j in range(4):
        send(vgall.at[h, j], vgall.at[h, j], ysem.at[0, j], c, yr, ygsem)
        jj = (j + 2) % 4
        send(vgall.at[h, jj], vgall.at[h, jj], ysem.at[1, jj], c, yl, ygsem)
    send(vgall.at[h, pl.ds(2 * (1 - kk), 2)], vsib.at[0], svsem.at[0], sib, h, fwsem)
    sent(vgall.at[pl.ds(0, 2)], ygsem)
    sent(vgall.at[0], yrsem)
    sent(vgall.at[pl.ds(0, 2)], fwsem)

    def pick(first, second):
        return jnp.where(kk == 0, first, second)

    origins = (h, pick(yl, yr), pick(yr, yl), yo, yo)
    sib_origins = (h, origins[2], origins[1], yo, yo)
    senders = (h, pick(yr, yl), pick(yl, yr), yo, yo)
    heads = ((0, 1), (0, 1), (0, 1), (0,), (1,))
    cols = tuple(128 * len(js) for js in heads)

    def forward(e):
        js = heads[e]
        send(vgall.at[sib_origins[e], pl.ds(2 * (1 - kk) + js[0], len(js))], vsib.at[e, pl.ds(0, len(js))],
             svsem.at[e], sib, h, fwsem)

    def pair(ref, at, j, n):
        if n == 1:
            return ref[at, j]
        return jnp.concatenate([ref[at, j], ref[at, j + 1]], axis=1)

    def partial(e):
        w = cols[e]

        def own(i, carry):
            rows = pl.ds(pl.multiple_of(256 * i, 256), 256)
            p = mm(int_[0, rows, :], pair(vgall, origins[e], 2 * kk + heads[e][0], len(heads[e])))
            b, x0 = i // 2, 2 * (i % 2)
            part[e, x0, b, :, :w] = p[:128]
            part[e, x0 + 1, b, :, :w] = p[128:]
            return carry

        def other(i, carry):
            rows = pl.ds(pl.multiple_of(256 * i, 256), 256)
            p = mm(int_[1, rows, :], pair(vsib, e, 0, len(heads[e])))
            b, x0 = i // 2, 2 * (i % 2)
            part[e, x0, b, :, :w] += p[:128]
            part[e, x0 + 1, b, :, :w] += p[128:]
            return carry

        lax.fori_loop(0, 4, own, 0)
        arrived(vsib.at[e, pl.ds(0, len(heads[e]))], svsem.at[e])
        lax.fori_loop(0, 4, other, 0)

    def ways(e):
        return (xr, xl) if e == 2 else (xl, xr)

    xgsem, zgsem, zfsem, xfsem = group(), group(), group(2), group(2)

    def cut(ref, e):
        return ref.at[e, :, :, pl.ds(0, cols[e])]

    def xsend1(e):
        fw, bw = ways(e)
        w = cols[e]
        sxa[e, :, :, :w] = part[e, (x + 2) % NX, :, :, :w].astype(BF16)
        send(cut(sxa, e), cut(rxa, e), xsem.at[0, e], cidx(z, fw, kk), h, xgsem)
        sxb[e, :, :, :w] = part[e, bw, :, :, :w].astype(BF16)
        send(cut(sxb, e), cut(rxb, e), xsem.at[1, e], cidx(z, bw, kk), h, xgsem)

    def xsend2(e):
        fw, bw = ways(e)
        w = cols[e]
        arrived(cut(rxa, e), xsem.at[0, e])
        sxc[e, :, :, :w] = (part[e, fw, :, :, :w] + rxa[e, :, :, :w].astype(F32)).astype(BF16)
        send(cut(sxc, e), cut(rxc, e), xsem.at[2, e], cidx(z, fw, kk), h, xgsem)

    def xdone(e):
        w = cols[e]
        arrived(cut(rxb, e), xsem.at[1, e])
        arrived(cut(rxc, e), xsem.at[2, e])
        for p in range(NZ):
            b, r0 = p % 2, 64 * (p // 2 % 2) + 32 * (p // 4)
            total = (part[e, x, b, r0:r0 + 32, :w] + rxb[e, b, r0:r0 + 32, :w].astype(F32)
                     + rxc[e, b, r0:r0 + 32, :w].astype(F32))
            zs[e, p, :, :w] = total.astype(BF16)
        for dz in (4, 3, 5, 2, 6, 1, 7, 0):
            to = (z + dz) % NZ
            send(zs.at[e, to, :, pl.ds(0, w)], zr.at[e, z, :, pl.ds(0, w)], zsem.at[e],
                 cidx(to, x, kk), origins[e], zgsem)

    mine = kk == z // 2 % 2
    slot = 2 * kk + z // 4

    def finish(e, total):
        w = cols[e]
        lo = 128 if e == 4 else 0
        fs[e, :, :w] = total * wscale
        to = cidx(2 * senders[e] + z % 2, x, z // 2 % 2)
        local = mine & (senders[e] == z // 2)
        remote = jnp.logical_not(local)
        pending.append((remote, send(fs.at[e, :, pl.ds(0, w)], fr.at[slot, :, pl.ds(lo, w)], fsem, to, h,
                                     group(), remote)))

        @pl.when(local)
        def _():
            fr[slot, :, lo:lo + w] = fs[e, :, :w]

    def zdone(e):
        w = cols[e]
        arrived(zr.at[e, :, :, pl.ds(0, w)], zsem.at[e])
        total = zr[e, 0, :, :w].astype(F32)
        for zz in range(1, NZ):
            total = total + zr[e, zz, :, :w].astype(F32)
        finish(e, total)

    def zfirst(e):
        for p in range(NZ):
            b, r0 = p % 2, 64 * (p // 2 % 2) + 32 * (p // 4)
            zfs[e, p] = part[e, :, b, r0:r0 + 32, :].astype(BF16)
        for dz in range(1, NZ):
            to = (z + dz) % NZ
            send(zfs.at[e, to], zfr.at[e, z], zsem.at[e], cidx(to, x, kk), h, zfsem[e])
        zfr[e, z] = zfs[e, z]
        sent(zfr.at[e, pl.ds(0, 7)], zfsem[e])

    def xnext(e):
        arrived(zfr.at[e, pl.ds(0, 7)], zsem.at[e])
        for xx in range(NX):
            total = zfr[e, 0, xx].astype(F32)
            for zz in range(1, NZ):
                total = total + zfr[e, zz, xx].astype(F32)
            xfs[e, xx] = total.astype(BF16)
        for dx in (2, 1, 3) if e == 0 else (2, 1, 3, 0):
            to = (x + dx) % NX
            send(xfs.at[e, to], xfr.at[e, x], xsem.at[0, e], cidx(z, to, kk), origins[e], xfsem[e])
        if e == 0:
            xfr[e, x] = xfs[e, x]
            sent(xfr.at[e, pl.ds(0, 3)], xfsem[e])
        else:
            sent(xfr.at[e], xfsem[e])

    def xlast(e):
        arrived(xfr.at[e, pl.ds(0, 3)] if e == 0 else xfr.at[e], xsem.at[0, e])
        total = xfr[e, 0].astype(F32)
        for xx in range(1, NX):
            total = total + xfr[e, xx].astype(F32)
        finish(e, total)

    def key_step(j, carry):
        at = pl.ds(pl.multiple_of(128 * j, 128), 128)
        ks[:, at] = (factor * (kloc[j] + mm(vh[j], later[j], NT))).astype(BF16)
        return carry

    def query_step(j, carry):
        at = pl.ds(pl.multiple_of(128 * j, 128), 128)
        qs[:, at] = (factor * (qloc[j] + mm(gh[j], prior[j], NT))).astype(BF16)
        return carry

    def put(src, dst, n):
        pltpu.make_async_copy(src, dst, osem.at[n]).start()

    xo = (x + 2) % NX

    def wblock(u, b, at):
        return wbuf.at[(h + u) % NY, b, at, kk]

    wxsem, wrsem, wssem = group(), group(), group()

    def wx(u):
        for b in range(2):
            send(wblock(u, b, x), wblock(u, b, x), w3sem.at[2 * b, u], cidx(z, xr, kk), h, wxsem)
            send(wblock(u, 1 - b, x), wblock(u, 1 - b, x), w3sem.at[1 + b, u], cidx(z, xl, kk), h, wxsem)

    def wrelay(u):
        arrived(wblock(u, 0, xl), w3sem.at[0, u])
        send(wblock(u, 0, xl), wblock(u, 0, xl), w3sem.at[3, u], cidx(z, xr, kk), h, wrsem)
        arrived(wblock(u, 1, xr), w3sem.at[1, u])
        send(wblock(u, 1, xr), wblock(u, 1, xr), w3sem.at[3, u], cidx(z, xl, kk), h, wrsem)

    def wsib(u, n):
        ref = wbuf.at[(h + u) % NY, :, (x, xl, xr, xo)[n], kk]
        send(ref, ref, w4sem.at[u], sib, h, wssem)

    def wneighbours(u):
        arrived(wbuf.at[(h + u) % NY, :, xl, kk], w3sem.at[2, u])
        wsib(u, 1)
        wsib(u, 2)

    def wopposite(u):
        arrived(wbuf.at[(h + u) % NY, :, xo, kk], w3sem.at[3, u])
        wsib(u, 3)

    def input_part(u):
        o = (h + u) % NY
        arrived(wbuf.at[o, :, :, 1 - kk], w4sem.at[u])

        def step(i, carry):
            b, x0 = i // 2, 2 * (i % 2)
            w = wbuf[o, b, pl.ds(x0, 2)].reshape(256, 512)
            p = mm(pair(vgall, o, 0, 2), w[:, :256], NT) + mm(pair(vgall, o, 2, 2), w[:, 256:], NT)
            if u == 3:
                ist[i] = (acc[i] + p).astype(BF16)
            else:
                acc[i] = p if u == 0 else acc[i] + p
            return carry
        lax.fori_loop(0, 4, step, 0)

    partial(0)
    zfirst(0)
    arrived(wz.at[pl.ds(0, 6)], w2sem)
    for u in range(NY):
        wx(u)
    scan3(wsk, z2k, zak, o3k, prior, 1, False)
    for u in range(NY):
        wsib(u, 0)
    transposed_part(vh, gh, qh, kloc)
    lax.fori_loop(0, 4, key_step, 0)
    put(ks, k_out, 0)

    for j in range(2):
        arrived(vgall.at[yl, j], ysem.at[0, j])
        send(vgall.at[yl, j], vgall.at[yl, j], ysem.at[2, j], c, yr, yrsem)
        arrived(vgall.at[yr, 2 + j], ysem.at[1, 2 + j])
        send(vgall.at[yr, 2 + j], vgall.at[yr, 2 + j], ysem.at[2, 2 + j], c, yl, yrsem)
    forward(1)
    partial(1)
    zfirst(1)
    wrelay(0)
    wrelay(1)
    straight_part(gh, vh, kh, qloc)

    for j in range(2):
        arrived(vgall.at[yl, 2 + j], ysem.at[0, 2 + j])
        arrived(vgall.at[yr, j], ysem.at[1, j])
    forward(2)
    partial(2)
    xsend1(2)

    for j in (0, 2):
        arrived(vgall.at[yo, j], ysem.at[2, j])
    forward(3)
    partial(3)
    xsend1(3)
    for j in (1, 3):
        arrived(vgall.at[yo, j], ysem.at[2, j])
    forward(4)
    partial(4)
    xsend1(4)
    xsend2(2)
    xnext(0)
    xsend2(3)
    scan_done(o3k, 1)
    lax.fori_loop(0, 4, query_step, 0)
    put(qs, q_out, 0)
    xsend2(4)
    xnext(1)
    wrelay(2)
    wrelay(3)
    wneighbours(0)
    wneighbours(1)
    wopposite(0)
    wopposite(1)
    xdone(2)
    xdone(3)
    input_part(0)
    xdone(4)
    xlast(0)
    input_part(1)
    xlast(1)
    zdone(2)
    wneighbours(2)
    wneighbours(3)
    wopposite(2)
    wopposite(3)
    zdone(3)
    zdone(4)
    input_part(2)
    input_part(3)
    for i in range(4):
        put(ist.at[i], i_out.at[:, pl.ds(256 * i, 256)], 1)
    sent(vgall.at[pl.ds(0, 2)], wxsem)
    sent(vgall.at[0], wrsem)
    sent(vgall, wssem)
    sent(vsib.at[pl.ds(0, 3)], xgsem)
    sent(zs.at[pl.ds(0, 2)], zgsem)

    @pl.when(mine)
    def _():
        arrived(fr.at[pl.ds(0, 3)], fsem)

    @pl.when(jnp.logical_not(mine))
    def _():
        arrived(fr, fsem)

    for n in range(4):
        put(fr.at[n], w_out.at[pl.ds(32 * (n % 2), 32), pl.ds(256 * (n // 2), 256)], 2)
    arrived(vgall.at[pl.ds(0, 2)], osem.at[0])
    arrived(ist, osem.at[1])
    arrived(fr, osem.at[2])
    for cond, desc in pending:
        if cond is None:
            desc.wait()
        else:
            pl.when(cond)(desc.wait_send)


def write_out(q_in, k_in, i_in, w_in, q_out, k_out, i_out, w_out, sems):
    pairs = ((i_in, i_out), (q_in, q_out), (k_in, k_out), (w_in, w_out))
    copies = [pltpu.make_async_copy(src, dst, sems.at[n]) for n, (src, dst) in enumerate(pairs)]
    for copy in copies:
        copy.start()
    for copy in copies:
        copy.wait()


def local(queries, keys, values, out_grad, inputs, value_weight):
    length = queries.shape[0]
    tokens = length * lax.axis_size("ctx")
    factor = 1.0 / math.sqrt(DH * tokens)
    wscale = 1.0 / math.sqrt(tokens)
    vm = pltpu.VMEM
    dma = pltpu.SemaphoreType.DMA
    scratch = [
        vm((4, 512, 128), BF16), vm((4, 512, 128), BF16), vm((4, 512, 128), BF16), vm((4, 512, 128), BF16),
        vm((2, 512, 1024), BF16), vm((2, 1024, 512), BF16),
        vm((8, 64, 512), BF16), vm((4, 2, 4, 2, 64, 512), BF16),
        vm((4, 128, 128), F32), vm((4, 128, 128), F32),
        vm((8, 64, 128), F32), vm((8, 64, 128), F32),
        vm((8, 64, 128), F32), vm((8, 64, 128), F32),
        vm((64, 128), BF16), vm((64, 128), BF16),
        vm((8, 64, 128), BF16), vm((8, 64, 128), BF16),
        vm((64, 128), F32), vm((64, 128), F32),
        vm((8, 64, 128), BF16), vm((8, 64, 128), BF16),
        vm((4, 128, 128), BF16), vm((4, 128, 128), BF16),
        vm((4, 512, 128), F32), vm((4, 512, 128), F32), vm((4, 512, 128), F32),
        vm((4, 4, 512, 128), BF16), vm((5, 2, 512, 128), BF16),
        vm((5, 4, 2, 128, 256), F32), vm((4, 512, 256), F32),
        vm((5, 2, 128, 256), BF16), vm((5, 2, 128, 256), BF16), vm((5, 2, 128, 256), BF16),
        vm((5, 2, 128, 256), BF16), vm((5, 2, 128, 256), BF16), vm((5, 2, 128, 256), BF16),
        vm((5, 8, 32, 256), BF16), vm((5, 8, 32, 256), BF16),
        vm((2, 8, 4, 32, 256), BF16), vm((2, 8, 4, 32, 256), BF16), vm((2, 4, 32, 256), BF16), vm((2, 4, 32, 256), BF16),
        vm((5, 32, 256), F32), vm((4, 32, 256), F32),
        vm((512, 512), BF16), vm((512, 512), BF16), vm((4, 512, 256), BF16),
        dma((6,)), dma((40,)), dma((2,)), dma((2, 8)), dma((2,)),
        dma((2, 5)), dma(()), dma((4, 4)), dma((4,)), dma(()), dma((3, 4)), dma((5,)), dma((3, 5)),
        dma((5,)), dma(()), dma((3,)),
    ]
    out_shape = (
        pltpu.VMEM((512, 512), BF16),
        pltpu.VMEM((512, 512), BF16),
        pltpu.VMEM((512, 1024), BF16),
        pltpu.VMEM((64, 512), F32),
    )
    results = pl.pallas_call(
        functools.partial(kernel, factor, wscale),
        out_shape=out_shape,
        in_specs=[pl.BlockSpec(memory_space=pl.ANY)] * 6,
        out_specs=[pl.BlockSpec(memory_space=pl.ANY)] * 4,
        scratch_shapes=scratch,
        compiler_params=pltpu.CompilerParams(
            collective_id=0, has_side_effects=True, vmem_limit_bytes=56 * 1024 * 1024),
        name="attention_backward",
    )(queries, keys, values, out_grad, inputs, value_weight)
    return pl.pallas_call(
        write_out,
        out_shape=tuple(jax.ShapeDtypeStruct(r.shape, r.dtype) for r in results),
        in_specs=[pl.BlockSpec(memory_space=pltpu.VMEM)] * 4,
        out_specs=[pl.BlockSpec(memory_space=pl.ANY)] * 4,
        scratch_shapes=[dma((4,))],
        name="write_out",
    )(*(pltpu.with_memory_space_constraint(r, pltpu.VMEM) for r in results))


def solution(mesh):
    spec = P("ctx", "head")
    return jax.shard_map(
        local, mesh=mesh, in_specs=(spec,) * 6, out_specs=(spec,) * 4, check_vma=False)
```

```python
import functools
import math

import jax
import jax.numpy as jnp
from jax import lax
from jax.experimental import pallas as pl
from jax.experimental.pallas import tpu as pltpu
from jax.sharding import PartitionSpec as P

DH = 128
NX, NZ, NC, NY = 4, 8, 2, 4
F32, BF16 = jnp.float32, jnp.bfloat16
MESH = pl.DeviceIdType.MESH
NT = (((1,), (1,)), ((), ()))
NN = (((1,), (0,)), ((), ()))


def mm(a, b, dims=NN):
    return lax.dot_general(a, b, dims, preferred_element_type=F32)


def kernel(
    factor, wscale,
    q_hbm, k_hbm, v_hbm, g_hbm, in_hbm, w_hbm,
    q_out, k_out, i_out, w_out,
    qh, kh, vh, gh, inb, int_, wz, wbuf,
    sq, sk, r1q, r1k, wsq, wsk, t2q, t2k, z2q, z2k, zaq, zak, o3q, o3k, later, prior,
    qloc, kloc, vloc, vgall, vsib, part, acc,
    sxa, sxb, sxc, rxa, rxb, rxc, zs, zr, zfs, zfr, xfs, xfr, fs, fr, qs, ks, ist,
    lsem, ssem, p1sem, p2sem, p3sem, w1sem, w2sem, w3sem, w4sem, isem, ysem, svsem, xsem, zsem, fsem, osem,
):
    c, h = lax.axis_index("ctx"), lax.axis_index("head")
    z, m = c // 8, c % 8
    x, kk = m // 2, m % 2

    def cidx(zz, xx, cc):
        return zz * 8 + xx * 2 + cc

    sib = cidx(z, x, 1 - kk)
    xr, xl = (x + 1) % NX, (x + 3) % NX
    yr, yl, yo = (h + 1) % NY, (h + 3) % NY, (h + 2) % NY

    pending = []
    count = [0]

    def group(n=1):
        count[0] += n
        return ssem.at[count[0] - n] if n == 1 else [ssem.at[count[0] - n + i] for i in range(n)]

    def send(src, dst, rsem, ctx, head, sem, cond=None):
        desc = pltpu.make_async_remote_copy(
            src_ref=src, dst_ref=dst, send_sem=sem, recv_sem=rsem,
            device_id=(ctx, head), device_id_type=MESH)
        if cond is None:
            desc.start()
        else:
            pl.when(cond)(desc.start)
        return desc

    def sent(ref, sem):
        pending.append((None, pltpu.make_async_copy(ref, ref, sem)))

    def arrived(dst, sem, cond=None):
        desc = pltpu.make_async_copy(dst, dst, sem)
        if cond is None:
            desc.wait()
        else:
            pl.when(cond)(desc.wait)

    for n, (src, dst) in enumerate(((q_hbm, qh), (g_hbm, gh), (k_hbm, kh), (v_hbm, vh))):
        for j in range(4):
            pltpu.make_async_copy(src.at[:, pl.ds(DH * j, DH)], dst.at[j], lsem.at[n]).start()
    load_w = pltpu.make_async_copy(w_hbm, wz.at[z], lsem.at[4])
    load_w.start()
    load_i = pltpu.make_async_copy(in_hbm, inb.at[0], lsem.at[5])
    load_i.start()

    barrier = pltpu.get_barrier_semaphore()
    partners = 0

    def greet(ctx, head):
        pl.semaphore_signal(barrier, inc=1, device_id=(ctx, head), device_id_type=MESH)

    for off in range(1, 8):
        mm_ = (m + off) % 8
        greet(z * 8 + mm_, h)
        partners += 1
    for off in range(1, 8):
        zz = (z + off) % NZ
        greet(cidx(zz, x, kk), h)
        partners += 1
    for off in range(1, 4):
        greet(c, (h + off) % NY)
        partners += 1

    arrived(qh, lsem.at[0])
    arrived(gh, lsem.at[1])
    for j in range(4):
        sq[j] = mm(qh[j].T, gh[j])
    arrived(kh, lsem.at[2])
    arrived(vh, lsem.at[3])
    for j in range(4):
        sk[j] = mm(kh[j].T, vh[j])
    pl.semaphore_wait(barrier, partners)

    plane = [2 * ((x + dx) % NX) + (kk + dk) % 2 for dx, dk in
             ((2, 0), (2, 1), (1, 0), (3, 0), (1, 1), (3, 1), (0, 1))]

    def scan1(s, r1, row):
        sem = group()
        for to in plane:
            send(s.at[to // 2, pl.ds(pl.multiple_of(64 * (to % 2), 64), 64)], r1.at[m],
                 p1sem.at[row], z * 8 + to, h, sem)
        sent(r1.at[pl.ds(0, 7)], sem)
        r1[m] = s[x, pl.ds(pl.multiple_of(64 * kk, 64), 64), :]

    def scan2(r1, ws, t2, z2, row, reverse):
        arrived(r1.at[pl.ds(0, 7)], p1sem.at[row])
        total = jnp.zeros((64, DH), F32)
        order = range(7, -1, -1) if reverse else range(8)
        for i in order:
            ws[i] = total
            total = total + r1[i]
        t2[...] = total.astype(BF16)
        for d in (4, 3, 5, 2, 6, 1, 7):
            zz = z - d if reverse else z + d
            cond = zz >= 0 if reverse else zz < NZ
            desc = send(t2, z2.at[d], p2sem.at[row, d], cidx(jnp.clip(zz, 0, NZ - 1), x, kk), h, group(), cond)
            pending.append((cond, desc))

    def scan3(ws, z2, za, o3, full, row, reverse):
        za[...] = jnp.zeros((64, DH), F32)
        for d in range(1, NZ):
            cond = z + d < NZ if reverse else z - d >= 0

            @pl.when(cond)
            def _():
                arrived(z2.at[d], p2sem.at[row, d])
                za[...] += z2[d].astype(F32)
        for i in range(8):
            o3[i] = (ws[i] + za[...]).astype(BF16)
        sem = group()
        for to in plane:
            send(o3.at[to], full.at[x, pl.ds(pl.multiple_of(64 * kk, 64), 64)],
                 p3sem.at[row], z * 8 + to, h, sem)
        sent(o3.at[pl.ds(0, 7)], sem)
        full[x, pl.ds(pl.multiple_of(64 * kk, 64), 64), :] = o3[m]

    def scan_done(o3, row):
        arrived(o3.at[pl.ds(0, 7)], p3sem.at[row])

    scan1(sq, r1q, 0)

    wnsem, wzsem = group(), group()

    def wnext(zs):
        to = zs // 2
        send(wz.at[zs], wbuf.at[h, zs % 2, x, kk], w2sem, c, to, wnsem, to != h)

        @pl.when(to == h)
        def _():
            wbuf[h, zs % 2, x, kk] = wz[zs]

    def wz_to(at, sem, dz):
        send(wz.at[at], wz.at[at], sem, cidx((z + dz + NZ) % NZ, x, kk), h, wzsem)

    def wring1():
        load_w.wait()
        for d in (2, 1):
            wz_to(z, w1sem.at[0, d], d)
            wz_to(z, w1sem.at[1, d], -d)
        wnext(z)

    def wring2():
        right, left = (z + 6) % NZ, (z + 2) % NZ
        arrived(wz.at[right], w1sem.at[0, 2])
        arrived(wz.at[left], w1sem.at[1, 2])
        wz_to(right, w1sem.at[0, 3], 1)
        wz_to(left, w1sem.at[1, 3], -1)
        wz_to(right, w1sem.at[0, 4], 2)
        wnext(right)
        wnext(left)

    def wring2b():
        for side, at in ((0, (z + 7) % NZ), (1, (z + 1) % NZ)):
            arrived(wz.at[at], w1sem.at[side, 1])
            wnext(at)

    def wring3():
        for side, d, at in ((0, 3, (z + 5) % NZ), (1, 3, (z + 3) % NZ), (0, 4, (z + 4) % NZ)):
            arrived(wz.at[at], w1sem.at[side, d])
            wnext(at)

    wring1()
    scan1(sk, r1k, 1)
    load_i.wait()
    insem = group()
    send(inb.at[0], inb.at[1], isem, sib, h, insem)
    sent(inb.at[0], insem)

    def masked_t(a, b, width):
        s = mm(a, b, NT)
        rows = lax.broadcasted_iota(jnp.int32, (256, width), 0)
        cols = lax.broadcasted_iota(jnp.int32, (256, width), 1)
        return jnp.where(rows <= cols, s, 0.0).astype(BF16)

    def transposed_part(a, b, c_, out):
        def step(j, carry):
            for i in range(2):
                lo = 256 * i
                s = masked_t(a[j, lo:lo + 256, :], b[j, lo:512, :], 512 - lo)
                out[j, lo:lo + 256, :] = mm(s, c_[j, lo:512, :])
            return carry
        lax.fori_loop(0, 4, step, 0)

    def straight_part(a, b, c_, out):
        def step(j, carry):
            for i in range(2):
                lo, hi = 256 * i, 256 * i + 256
                s = mm(a[j, lo:hi, :], b[j, 0:hi, :], NT)
                rows = lax.broadcasted_iota(jnp.int32, (256, hi), 0) + lo
                cols = lax.broadcasted_iota(jnp.int32, (256, hi), 1)
                s = jnp.where(rows >= cols, s, 0.0).astype(BF16)
                out[j, lo:hi, :] = mm(s, c_[j, 0:hi, :])
            return carry
        lax.fori_loop(0, 4, step, 0)

    def transpose_inputs(slot):
        def step(j, carry):
            at = pl.multiple_of(128 * j, 128)
            int_[slot, pl.ds(at, 128), :] = inb[slot, :, pl.ds(at, 128)].T
            return carry
        lax.fori_loop(0, 8, step, 0)

    sent(wz.at[pl.ds(0, 6)], wnsem)
    sent(wz.at[pl.ds(0, 7)], wzsem)
    scan2(r1q, wsq, t2q, z2q, 0, True)
    wring2()
    transposed_part(kh, qh, gh, vloc)
    wring2b()
    scan2(r1k, wsk, t2k, z2k, 1, False)
    transpose_inputs(0)
    arrived(inb.at[1], isem)
    transpose_inputs(1)
    scan3(wsq, z2q, zaq, o3q, later, 0, True)
    wring3()

    scan_done(o3q, 0)
    for j in range(4):
        val = factor * (vloc[j] + mm(kh[j], later[j]))
        vgall[h, j] = val.astype(BF16)
    ygsem, yrsem, fwsem = group(), group(), group()
    for j in range(4):
        send(vgall.at[h, j], vgall.at[h, j], ysem.at[0, j], c, yr, ygsem)
        jj = (j + 2) % 4
        send(vgall.at[h, jj], vgall.at[h, jj], ysem.at[1, jj], c, yl, ygsem)
    send(vgall.at[h, pl.ds(2 * (1 - kk), 2)], vsib.at[0], svsem.at[0], sib, h, fwsem)
    sent(vgall.at[pl.ds(0, 2)], ygsem)
    sent(vgall.at[0], yrsem)
    sent(vgall.at[pl.ds(0, 2)], fwsem)

    def pick(first, second):
        return jnp.where(kk == 0, first, second)

    origins = (h, pick(yl, yr), pick(yr, yl), yo, yo)
    sib_origins = (h, origins[2], origins[1], yo, yo)
    senders = (h, pick(yr, yl), pick(yl, yr), yo, yo)
    heads = ((0, 1), (0, 1), (0, 1), (0,), (1,))
    cols = tuple(128 * len(js) for js in heads)

    def forward(e):
        js = heads[e]
        send(vgall.at[sib_origins[e], pl.ds(2 * (1 - kk) + js[0], len(js))], vsib.at[e, pl.ds(0, len(js))],
             svsem.at[e], sib, h, fwsem)

    def pair(ref, at, j, n):
        if n == 1:
            return ref[at, j]
        return jnp.concatenate([ref[at, j], ref[at, j + 1]], axis=1)

    def partial(e):
        w = cols[e]

        def own(i, carry):
            rows = pl.ds(pl.multiple_of(256 * i, 256), 256)
            p = mm(int_[0, rows, :], pair(vgall, origins[e], 2 * kk + heads[e][0], len(heads[e])))
            b, x0 = i // 2, 2 * (i % 2)
            part[e, x0, b, :, :w] = p[:128]
            part[e, x0 + 1, b, :, :w] = p[128:]
            return carry

        def other(i, carry):
            rows = pl.ds(pl.multiple_of(256 * i, 256), 256)
            p = mm(int_[1, rows, :], pair(vsib, e, 0, len(heads[e])))
            b, x0 = i // 2, 2 * (i % 2)
            part[e, x0, b, :, :w] += p[:128]
            part[e, x0 + 1, b, :, :w] += p[128:]
            return carry

        lax.fori_loop(0, 4, own, 0)
        arrived(vsib.at[e, pl.ds(0, len(heads[e]))], svsem.at[e])
        lax.fori_loop(0, 4, other, 0)

    def ways(e):
        return (xr, xl) if e == 2 else (xl, xr)

    xgsem, zgsem, zfsem, xfsem = group(), group(), group(2), group(2)

    def cut(ref, e):
        return ref.at[e, :, :, pl.ds(0, cols[e])]

    def xsend1(e):
        fw, bw = ways(e)
        w = cols[e]
        sxa[e, :, :, :w] = part[e, (x + 2) % NX, :, :, :w].astype(BF16)
        send(cut(sxa, e), cut(rxa, e), xsem.at[0, e], cidx(z, fw, kk), h, xgsem)
        sxb[e, :, :, :w] = part[e, bw, :, :, :w].astype(BF16)
        send(cut(sxb, e), cut(rxb, e), xsem.at[1, e], cidx(z, bw, kk), h, xgsem)

    def xsend2(e):
        fw, bw = ways(e)
        w = cols[e]
        arrived(cut(rxa, e), xsem.at[0, e])
        sxc[e, :, :, :w] = (part[e, fw, :, :, :w] + rxa[e, :, :, :w].astype(F32)).astype(BF16)
        send(cut(sxc, e), cut(rxc, e), xsem.at[2, e], cidx(z, fw, kk), h, xgsem)

    def xdone(e):
        w = cols[e]
        arrived(cut(rxb, e), xsem.at[1, e])
        arrived(cut(rxc, e), xsem.at[2, e])
        for p in range(NZ):
            b, r0 = p % 2, 64 * (p // 2 % 2) + 32 * (p // 4)
            total = (part[e, x, b, r0:r0 + 32, :w] + rxb[e, b, r0:r0 + 32, :w].astype(F32)
                     + rxc[e, b, r0:r0 + 32, :w].astype(F32))
            zs[e, p, :, :w] = total.astype(BF16)
        for dz in (4, 3, 5, 2, 6, 1, 7, 0):
            to = (z + dz) % NZ
            send(zs.at[e, to, :, pl.ds(0, w)], zr.at[e, z, :, pl.ds(0, w)], zsem.at[e],
                 cidx(to, x, kk), origins[e], zgsem)

    mine = kk == z // 2 % 2
    slot = 2 * kk + z // 4

    def finish(e, total):
        w = cols[e]
        lo = 128 if e == 4 else 0
        fs[e, :, :w] = total * wscale
        to = cidx(2 * senders[e] + z % 2, x, z // 2 % 2)
        local = mine & (senders[e] == z // 2)
        remote = jnp.logical_not(local)
        pending.append((remote, send(fs.at[e, :, pl.ds(0, w)], fr.at[slot, :, pl.ds(lo, w)], fsem, to, h,
                                     group(), remote)))

        @pl.when(local)
        def _():
            fr[slot, :, lo:lo + w] = fs[e, :, :w]

    def zdone(e):
        w = cols[e]
        arrived(zr.at[e, :, :, pl.ds(0, w)], zsem.at[e])
        total = zr[e, 0, :, :w].astype(F32)
        for zz in range(1, NZ):
            total = total + zr[e, zz, :, :w].astype(F32)
        finish(e, total)

    def zfirst(e):
        for p in range(NZ):
            b, r0 = p % 2, 64 * (p // 2 % 2) + 32 * (p // 4)
            zfs[e, p] = part[e, :, b, r0:r0 + 32, :].astype(BF16)
        for dz in range(1, NZ):
            to = (z + dz) % NZ
            send(zfs.at[e, to], zfr.at[e, z], zsem.at[e], cidx(to, x, kk), h, zfsem[e])
        zfr[e, z] = zfs[e, z]
        sent(zfr.at[e, pl.ds(0, 7)], zfsem[e])

    def xnext(e):
        arrived(zfr.at[e, pl.ds(0, 7)], zsem.at[e])
        for xx in range(NX):
            total = zfr[e, 0, xx].astype(F32)
            for zz in range(1, NZ):
                total = total + zfr[e, zz, xx].astype(F32)
            xfs[e, xx] = total.astype(BF16)
        for dx in (2, 1, 3) if e == 0 else (2, 1, 3, 0):
            to = (x + dx) % NX
            send(xfs.at[e, to], xfr.at[e, x], xsem.at[0, e], cidx(z, to, kk), origins[e], xfsem[e])
        if e == 0:
            xfr[e, x] = xfs[e, x]
            sent(xfr.at[e, pl.ds(0, 3)], xfsem[e])
        else:
            sent(xfr.at[e], xfsem[e])

    def xlast(e):
        arrived(xfr.at[e, pl.ds(0, 3)] if e == 0 else xfr.at[e], xsem.at[0, e])
        total = xfr[e, 0].astype(F32)
        for xx in range(1, NX):
            total = total + xfr[e, xx].astype(F32)
        finish(e, total)

    def key_step(j, carry):
        at = pl.ds(pl.multiple_of(128 * j, 128), 128)
        ks[:, at] = (factor * (kloc[j] + mm(vh[j], later[j], NT))).astype(BF16)
        return carry

    def query_step(j, carry):
        at = pl.ds(pl.multiple_of(128 * j, 128), 128)
        qs[:, at] = (factor * (qloc[j] + mm(gh[j], prior[j], NT))).astype(BF16)
        return carry

    def put(src, dst, n):
        pltpu.make_async_copy(src, dst, osem.at[n]).start()

    xo = (x + 2) % NX

    def wblock(u, b, at):
        return wbuf.at[(h + u) % NY, b, at, kk]

    wxsem, wrsem, wssem = group(), group(), group()

    def wx(u):
        for b in range(2):
            send(wblock(u, b, x), wblock(u, b, x), w3sem.at[2 * b, u], cidx(z, xr, kk), h, wxsem)
            send(wblock(u, 1 - b, x), wblock(u, 1 - b, x), w3sem.at[1 + b, u], cidx(z, xl, kk), h, wxsem)

    def wrelay(u):
        arrived(wblock(u, 0, xl), w3sem.at[0, u])
        send(wblock(u, 0, xl), wblock(u, 0, xl), w3sem.at[3, u], cidx(z, xr, kk), h, wrsem)
        arrived(wblock(u, 1, xr), w3sem.at[1, u])
        send(wblock(u, 1, xr), wblock(u, 1, xr), w3sem.at[3, u], cidx(z, xl, kk), h, wrsem)

    def wsib(u, n):
        ref = wbuf.at[(h + u) % NY, :, (x, xl, xr, xo)[n], kk]
        send(ref, ref, w4sem.at[u], sib, h, wssem)

    def wneighbours(u):
        arrived(wbuf.at[(h + u) % NY, :, xl, kk], w3sem.at[2, u])
        wsib(u, 1)
        wsib(u, 2)

    def wopposite(u):
        arrived(wbuf.at[(h + u) % NY, :, xo, kk], w3sem.at[3, u])
        wsib(u, 3)

    def input_part(u):
        o = (h + u) % NY
        arrived(wbuf.at[o, :, :, 1 - kk], w4sem.at[u])

        def step(i, carry):
            b, x0 = i // 2, 2 * (i % 2)
            w = wbuf[o, b, pl.ds(x0, 2)].reshape(256, 512)
            p = mm(pair(vgall, o, 0, 2), w[:, :256], NT) + mm(pair(vgall, o, 2, 2), w[:, 256:], NT)
            if u == 3:
                ist[i] = (acc[i] + p).astype(BF16)
            else:
                acc[i] = p if u == 0 else acc[i] + p
            return carry
        lax.fori_loop(0, 4, step, 0)

    partial(0)
    zfirst(0)
    arrived(wz.at[pl.ds(0, 6)], w2sem)
    for u in range(NY):
        wx(u)
    scan3(wsk, z2k, zak, o3k, prior, 1, False)
    for u in range(NY):
        wsib(u, 0)
    transposed_part(vh, gh, qh, kloc)
    lax.fori_loop(0, 4, key_step, 0)
    put(ks, k_out, 0)

    for j in range(2):
        arrived(vgall.at[yl, j], ysem.at[0, j])
        send(vgall.at[yl, j], vgall.at[yl, j], ysem.at[2, j], c, yr, yrsem)
        arrived(vgall.at[yr, 2 + j], ysem.at[1, 2 + j])
        send(vgall.at[yr, 2 + j], vgall.at[yr, 2 + j], ysem.at[2, 2 + j], c, yl, yrsem)
    forward(1)
    partial(1)
    zfirst(1)
    wrelay(0)
    wrelay(1)
    straight_part(gh, vh, kh, qloc)

    for j in range(2):
        arrived(vgall.at[yl, 2 + j], ysem.at[0, 2 + j])
        arrived(vgall.at[yr, j], ysem.at[1, j])
    forward(2)
    partial(2)
    xsend1(2)

    for j in (0, 2):
        arrived(vgall.at[yo, j], ysem.at[2, j])
    forward(3)
    partial(3)
    xsend1(3)
    for j in (1, 3):
        arrived(vgall.at[yo, j], ysem.at[2, j])
    forward(4)
    partial(4)
    xsend1(4)
    xsend2(2)
    xnext(0)
    xsend2(3)
    scan_done(o3k, 1)
    lax.fori_loop(0, 4, query_step, 0)
    put(qs, q_out, 0)
    for u in range(2):
        wneighbours(u)
        wopposite(u)
    xsend2(4)
    input_part(0)
    xdone(2)
    xdone(3)
    xlast(0)
    xnext(1)
    wrelay(2)
    wrelay(3)
    xdone(4)
    input_part(1)
    wneighbours(2)
    wneighbours(3)
    xlast(1)
    wopposite(2)
    wopposite(3)
    zdone(2)
    input_part(2)
    zdone(3)
    zdone(4)
    input_part(3)
    for i in range(4):
        put(ist.at[i], i_out.at[:, pl.ds(256 * i, 256)], 1)
    sent(vgall.at[pl.ds(0, 2)], wxsem)
    sent(vgall.at[0], wrsem)
    sent(vgall, wssem)
    sent(vsib.at[pl.ds(0, 3)], xgsem)
    sent(zs.at[pl.ds(0, 2)], zgsem)

    @pl.when(mine)
    def _():
        arrived(fr.at[pl.ds(0, 3)], fsem)

    @pl.when(jnp.logical_not(mine))
    def _():
        arrived(fr, fsem)

    for n in range(4):
        put(fr.at[n], w_out.at[pl.ds(32 * (n % 2), 32), pl.ds(256 * (n // 2), 256)], 2)
    arrived(vgall.at[pl.ds(0, 2)], osem.at[0])
    arrived(ist, osem.at[1])
    arrived(fr, osem.at[2])
    for cond, desc in pending:
        if cond is None:
            desc.wait()
        else:
            pl.when(cond)(desc.wait_send)


def write_out(q_in, k_in, i_in, w_in, q_out, k_out, i_out, w_out, sems):
    pairs = ((i_in, i_out), (q_in, q_out), (k_in, k_out), (w_in, w_out))
    copies = [pltpu.make_async_copy(src, dst, sems.at[n]) for n, (src, dst) in enumerate(pairs)]
    for copy in copies:
        copy.start()
    for copy in copies:
        copy.wait()


def local(queries, keys, values, out_grad, inputs, value_weight):
    length = queries.shape[0]
    tokens = length * lax.axis_size("ctx")
    factor = 1.0 / math.sqrt(DH * tokens)
    wscale = 1.0 / math.sqrt(tokens)
    vm = pltpu.VMEM
    dma = pltpu.SemaphoreType.DMA
    scratch = [
        vm((4, 512, 128), BF16), vm((4, 512, 128), BF16), vm((4, 512, 128), BF16), vm((4, 512, 128), BF16),
        vm((2, 512, 1024), BF16), vm((2, 1024, 512), BF16),
        vm((8, 64, 512), BF16), vm((4, 2, 4, 2, 64, 512), BF16),
        vm((4, 128, 128), F32), vm((4, 128, 128), F32),
        vm((8, 64, 128), F32), vm((8, 64, 128), F32),
        vm((8, 64, 128), F32), vm((8, 64, 128), F32),
        vm((64, 128), BF16), vm((64, 128), BF16),
        vm((8, 64, 128), BF16), vm((8, 64, 128), BF16),
        vm((64, 128), F32), vm((64, 128), F32),
        vm((8, 64, 128), BF16), vm((8, 64, 128), BF16),
        vm((4, 128, 128), BF16), vm((4, 128, 128), BF16),
        vm((4, 512, 128), F32), vm((4, 512, 128), F32), vm((4, 512, 128), F32),
        vm((4, 4, 512, 128), BF16), vm((5, 2, 512, 128), BF16),
        vm((5, 4, 2, 128, 256), F32), vm((4, 512, 256), F32),
        vm((5, 2, 128, 256), BF16), vm((5, 2, 128, 256), BF16), vm((5, 2, 128, 256), BF16),
        vm((5, 2, 128, 256), BF16), vm((5, 2, 128, 256), BF16), vm((5, 2, 128, 256), BF16),
        vm((5, 8, 32, 256), BF16), vm((5, 8, 32, 256), BF16),
        vm((2, 8, 4, 32, 256), BF16), vm((2, 8, 4, 32, 256), BF16), vm((2, 4, 32, 256), BF16), vm((2, 4, 32, 256), BF16),
        vm((5, 32, 256), F32), vm((4, 32, 256), F32),
        vm((512, 512), BF16), vm((512, 512), BF16), vm((4, 512, 256), BF16),
        dma((6,)), dma((40,)), dma((2,)), dma((2, 8)), dma((2,)),
        dma((2, 5)), dma(()), dma((4, 4)), dma((4,)), dma(()), dma((3, 4)), dma((5,)), dma((3, 5)),
        dma((5,)), dma(()), dma((3,)),
    ]
    out_shape = (
        pltpu.VMEM((512, 512), BF16),
        pltpu.VMEM((512, 512), BF16),
        pltpu.VMEM((512, 1024), BF16),
        pltpu.VMEM((64, 512), F32),
    )
    results = pl.pallas_call(
        functools.partial(kernel, factor, wscale),
        out_shape=out_shape,
        in_specs=[pl.BlockSpec(memory_space=pl.ANY)] * 6,
        out_specs=[pl.BlockSpec(memory_space=pl.ANY)] * 4,
        scratch_shapes=scratch,
        compiler_params=pltpu.CompilerParams(
            collective_id=0, has_side_effects=True, vmem_limit_bytes=56 * 1024 * 1024),
        name="attention_backward",
    )(queries, keys, values, out_grad, inputs, value_weight)
    return pl.pallas_call(
        write_out,
        out_shape=tuple(jax.ShapeDtypeStruct(r.shape, r.dtype) for r in results),
        in_specs=[pl.BlockSpec(memory_space=pltpu.VMEM)] * 4,
        out_specs=[pl.BlockSpec(memory_space=pl.ANY)] * 4,
        scratch_shapes=[dma((4,))],
        name="write_out",
    )(*(pltpu.with_memory_space_constraint(r, pltpu.VMEM) for r in results))


def solution(mesh):
    spec = P("ctx", "head")
    return jax.shard_map(
        local, mesh=mesh, in_specs=(spec,) * 6, out_specs=(spec,) * 4, check_vma=False)
```

```python
import functools
import math

import jax
import jax.numpy as jnp
from jax import lax
from jax.experimental import pallas as pl
from jax.experimental.pallas import tpu as pltpu
from jax.sharding import PartitionSpec as P

DH = 128
NX, NZ, NC, NY = 4, 8, 2, 4
F32, BF16 = jnp.float32, jnp.bfloat16
MESH = pl.DeviceIdType.MESH
NT = (((1,), (1,)), ((), ()))
NN = (((1,), (0,)), ((), ()))


def mm(a, b, dims=NN):
    return lax.dot_general(a, b, dims, preferred_element_type=F32)


def kernel(
    factor, wscale,
    q_hbm, k_hbm, v_hbm, g_hbm, in_hbm, w_hbm,
    q_out, k_out, i_out, w_out,
    qh, kh, vh, gh, inb, int_, wz, wbuf,
    sq, sk, r1q, r1k, wsq, wsk, t2q, t2k, z2q, z2k, zaq, zak, o3q, o3k, later, prior,
    qloc, kloc, vloc, vgall, vsib, part, acc,
    sxa, sxb, sxc, rxa, rxb, rxc, zs, zr, zfs, zfr, xfs, xfr, fs, fr, qs, ks, ist,
    lsem, ssem, p1sem, p2sem, p3sem, w1sem, w2sem, w3sem, w4sem, isem, ysem, svsem, xsem, zsem, fsem, osem,
):
    c, h = lax.axis_index("ctx"), lax.axis_index("head")
    z, m = c // 8, c % 8
    x, kk = m // 2, m % 2

    def cidx(zz, xx, cc):
        return zz * 8 + xx * 2 + cc

    sib = cidx(z, x, 1 - kk)
    xr, xl = (x + 1) % NX, (x + 3) % NX
    yr, yl, yo = (h + 1) % NY, (h + 3) % NY, (h + 2) % NY

    pending = []
    count = [0]

    def group(n=1):
        count[0] += n
        return ssem.at[count[0] - n] if n == 1 else [ssem.at[count[0] - n + i] for i in range(n)]

    def send(src, dst, rsem, ctx, head, sem, cond=None):
        desc = pltpu.make_async_remote_copy(
            src_ref=src, dst_ref=dst, send_sem=sem, recv_sem=rsem,
            device_id=(ctx, head), device_id_type=MESH)
        if cond is None:
            desc.start()
        else:
            pl.when(cond)(desc.start)
        return desc

    def sent(ref, sem):
        pending.append((None, pltpu.make_async_copy(ref, ref, sem)))

    def arrived(dst, sem, cond=None):
        desc = pltpu.make_async_copy(dst, dst, sem)
        if cond is None:
            desc.wait()
        else:
            pl.when(cond)(desc.wait)

    for n, (src, dst) in enumerate(((q_hbm, qh), (g_hbm, gh), (k_hbm, kh), (v_hbm, vh))):
        for j in range(4):
            pltpu.make_async_copy(src.at[:, pl.ds(DH * j, DH)], dst.at[j], lsem.at[n]).start()
    load_w = pltpu.make_async_copy(w_hbm, wz.at[z], lsem.at[4])
    load_w.start()
    load_i = pltpu.make_async_copy(in_hbm, inb.at[0], lsem.at[5])
    load_i.start()

    barrier = pltpu.get_barrier_semaphore()
    partners = 0

    def greet(ctx, head):
        pl.semaphore_signal(barrier, inc=1, device_id=(ctx, head), device_id_type=MESH)

    for off in range(1, 8):
        mm_ = (m + off) % 8
        greet(z * 8 + mm_, h)
        partners += 1
    for off in range(1, 8):
        zz = (z + off) % NZ
        greet(cidx(zz, x, kk), h)
        partners += 1
    for off in range(1, 4):
        greet(c, (h + off) % NY)
        partners += 1

    arrived(qh, lsem.at[0])
    arrived(gh, lsem.at[1])
    for j in range(4):
        sq[j] = mm(qh[j].T, gh[j])
    arrived(kh, lsem.at[2])
    arrived(vh, lsem.at[3])
    for j in range(4):
        sk[j] = mm(kh[j].T, vh[j])
    pl.semaphore_wait(barrier, partners)

    plane = [2 * ((x + dx) % NX) + (kk + dk) % 2 for dx, dk in
             ((2, 0), (2, 1), (1, 0), (3, 0), (1, 1), (3, 1), (0, 1))]

    def scan1(s, r1, row):
        sem = group()
        for to in plane:
            send(s.at[to // 2, pl.ds(pl.multiple_of(64 * (to % 2), 64), 64)], r1.at[m],
                 p1sem.at[row], z * 8 + to, h, sem)
        sent(r1.at[pl.ds(0, 7)], sem)
        r1[m] = s[x, pl.ds(pl.multiple_of(64 * kk, 64), 64), :]

    def scan2(r1, ws, t2, z2, row, reverse):
        arrived(r1.at[pl.ds(0, 7)], p1sem.at[row])
        total = jnp.zeros((64, DH), F32)
        order = range(7, -1, -1) if reverse else range(8)
        for i in order:
            ws[i] = total
            total = total + r1[i]
        t2[...] = total.astype(BF16)
        for d in (4, 3, 5, 2, 6, 1, 7):
            zz = z - d if reverse else z + d
            cond = zz >= 0 if reverse else zz < NZ
            desc = send(t2, z2.at[d], p2sem.at[row, d], cidx(jnp.clip(zz, 0, NZ - 1), x, kk), h, group(), cond)
            pending.append((cond, desc))

    def scan3(ws, z2, za, o3, full, row, reverse):
        za[...] = jnp.zeros((64, DH), F32)
        for d in range(1, NZ):
            cond = z + d < NZ if reverse else z - d >= 0

            @pl.when(cond)
            def _():
                arrived(z2.at[d], p2sem.at[row, d])
                za[...] += z2[d].astype(F32)
        for i in range(8):
            o3[i] = (ws[i] + za[...]).astype(BF16)
        sem = group()
        for to in plane:
            send(o3.at[to], full.at[x, pl.ds(pl.multiple_of(64 * kk, 64), 64)],
                 p3sem.at[row], z * 8 + to, h, sem)
        sent(o3.at[pl.ds(0, 7)], sem)
        full[x, pl.ds(pl.multiple_of(64 * kk, 64), 64), :] = o3[m]

    def scan_done(o3, row):
        arrived(o3.at[pl.ds(0, 7)], p3sem.at[row])

    scan1(sq, r1q, 0)

    wnsem, wzsem = group(), group()

    def wnext(zs):
        to = zs // 2
        send(wz.at[zs], wbuf.at[h, zs % 2, x, kk], w2sem, c, to, wnsem, to != h)

        @pl.when(to == h)
        def _():
            wbuf[h, zs % 2, x, kk] = wz[zs]

    def wz_to(at, sem, dz):
        send(wz.at[at], wz.at[at], sem, cidx((z + dz + NZ) % NZ, x, kk), h, wzsem)

    def wring1():
        load_w.wait()
        for d in (2, 1):
            wz_to(z, w1sem.at[0, d], d)
            wz_to(z, w1sem.at[1, d], -d)
        wnext(z)

    def wring2():
        right, left = (z + 6) % NZ, (z + 2) % NZ
        arrived(wz.at[right], w1sem.at[0, 2])
        arrived(wz.at[left], w1sem.at[1, 2])
        wz_to(right, w1sem.at[0, 3], 1)
        wz_to(left, w1sem.at[1, 3], -1)
        wz_to(right, w1sem.at[0, 4], 2)
        wnext(right)
        wnext(left)

    def wring2b():
        for side, at in ((0, (z + 7) % NZ), (1, (z + 1) % NZ)):
            arrived(wz.at[at], w1sem.at[side, 1])
            wnext(at)

    def wring3():
        for side, d, at in ((0, 3, (z + 5) % NZ), (1, 3, (z + 3) % NZ), (0, 4, (z + 4) % NZ)):
            arrived(wz.at[at], w1sem.at[side, d])
            wnext(at)

    wring1()
    scan1(sk, r1k, 1)
    load_i.wait()
    insem = group()
    send(inb.at[0], inb.at[1], isem, sib, h, insem)
    sent(inb.at[0], insem)

    def masked_t(a, b, width):
        s = mm(a, b, NT)
        rows = lax.broadcasted_iota(jnp.int32, (256, width), 0)
        cols = lax.broadcasted_iota(jnp.int32, (256, width), 1)
        return jnp.where(rows <= cols, s, 0.0).astype(BF16)

    def transposed_part(a, b, c_, out):
        def step(j, carry):
            for i in range(2):
                lo = 256 * i
                s = masked_t(a[j, lo:lo + 256, :], b[j, lo:512, :], 512 - lo)
                out[j, lo:lo + 256, :] = mm(s, c_[j, lo:512, :])
            return carry
        lax.fori_loop(0, 4, step, 0)

    def straight_part(a, b, c_, out):
        def step(j, carry):
            for i in range(2):
                lo, hi = 256 * i, 256 * i + 256
                s = mm(a[j, lo:hi, :], b[j, 0:hi, :], NT)
                rows = lax.broadcasted_iota(jnp.int32, (256, hi), 0) + lo
                cols = lax.broadcasted_iota(jnp.int32, (256, hi), 1)
                s = jnp.where(rows >= cols, s, 0.0).astype(BF16)
                out[j, lo:hi, :] = mm(s, c_[j, 0:hi, :])
            return carry
        lax.fori_loop(0, 4, step, 0)

    def transpose_inputs(slot):
        def step(j, carry):
            at = pl.multiple_of(128 * j, 128)
            int_[slot, pl.ds(at, 128), :] = inb[slot, :, pl.ds(at, 128)].T
            return carry
        lax.fori_loop(0, 8, step, 0)

    sent(wz.at[pl.ds(0, 6)], wnsem)
    sent(wz.at[pl.ds(0, 7)], wzsem)
    scan2(r1q, wsq, t2q, z2q, 0, True)
    wring2()
    transposed_part(kh, qh, gh, vloc)
    wring2b()
    scan2(r1k, wsk, t2k, z2k, 1, False)
    transpose_inputs(0)
    arrived(inb.at[1], isem)
    transpose_inputs(1)
    scan3(wsq, z2q, zaq, o3q, later, 0, True)
    wring3()

    scan_done(o3q, 0)
    for j in range(4):
        val = factor * (vloc[j] + mm(kh[j], later[j]))
        vgall[h, j] = val.astype(BF16)
    ygsem, yrsem, fwsem = group(), group(), group()
    for j in range(4):
        send(vgall.at[h, j], vgall.at[h, j], ysem.at[0, j], c, yr, ygsem)
        jj = (j + 2) % 4
        send(vgall.at[h, jj], vgall.at[h, jj], ysem.at[1, jj], c, yl, ygsem)
    send(vgall.at[h, pl.ds(2 * (1 - kk), 2)], vsib.at[0], svsem.at[0], sib, h, fwsem)
    sent(vgall.at[pl.ds(0, 2)], ygsem)
    sent(vgall.at[0], yrsem)
    sent(vgall.at[pl.ds(0, 2)], fwsem)

    def pick(first, second):
        return jnp.where(kk == 0, first, second)

    origins = (h, pick(yl, yr), pick(yr, yl), yo, yo)
    sib_origins = (h, origins[2], origins[1], yo, yo)
    senders = (h, pick(yr, yl), pick(yl, yr), yo, yo)
    heads = ((0, 1), (0, 1), (0, 1), (0,), (1,))
    cols = tuple(128 * len(js) for js in heads)

    def forward(e):
        js = heads[e]
        send(vgall.at[sib_origins[e], pl.ds(2 * (1 - kk) + js[0], len(js))], vsib.at[e, pl.ds(0, len(js))],
             svsem.at[e], sib, h, fwsem)

    def pair(ref, at, j, n):
        if n == 1:
            return ref[at, j]
        return jnp.concatenate([ref[at, j], ref[at, j + 1]], axis=1)

    def partial(e):
        w = cols[e]

        def own(i, carry):
            rows = pl.ds(pl.multiple_of(256 * i, 256), 256)
            p = mm(int_[0, rows, :], pair(vgall, origins[e], 2 * kk + heads[e][0], len(heads[e])))
            b, x0 = i // 2, 2 * (i % 2)
            part[e, x0, b, :, :w] = p[:128]
            part[e, x0 + 1, b, :, :w] = p[128:]
            return carry

        def other(i, carry):
            rows = pl.ds(pl.multiple_of(256 * i, 256), 256)
            p = mm(int_[1, rows, :], pair(vsib, e, 0, len(heads[e])))
            b, x0 = i // 2, 2 * (i % 2)
            part[e, x0, b, :, :w] += p[:128]
            part[e, x0 + 1, b, :, :w] += p[128:]
            return carry

        lax.fori_loop(0, 4, own, 0)
        arrived(vsib.at[e, pl.ds(0, len(heads[e]))], svsem.at[e])
        lax.fori_loop(0, 4, other, 0)

    def ways(e):
        return (xr, xl) if e == 2 else (xl, xr)

    xgsem, zgsem, zfsem, xfsem = group(), group(), group(2), group(2)

    def cut(ref, e):
        return ref.at[e, :, :, pl.ds(0, cols[e])]

    def xsend1(e):
        fw, bw = ways(e)
        w = cols[e]
        sxa[e, :, :, :w] = part[e, (x + 2) % NX, :, :, :w].astype(BF16)
        send(cut(sxa, e), cut(rxa, e), xsem.at[0, e], cidx(z, fw, kk), h, xgsem)
        sxb[e, :, :, :w] = part[e, bw, :, :, :w].astype(BF16)
        send(cut(sxb, e), cut(rxb, e), xsem.at[1, e], cidx(z, bw, kk), h, xgsem)

    def xsend2(e):
        fw, bw = ways(e)
        w = cols[e]
        arrived(cut(rxa, e), xsem.at[0, e])
        sxc[e, :, :, :w] = (part[e, fw, :, :, :w] + rxa[e, :, :, :w].astype(F32)).astype(BF16)
        send(cut(sxc, e), cut(rxc, e), xsem.at[2, e], cidx(z, fw, kk), h, xgsem)

    def xdone(e):
        w = cols[e]
        arrived(cut(rxb, e), xsem.at[1, e])
        arrived(cut(rxc, e), xsem.at[2, e])
        for p in range(NZ):
            b, r0 = p % 2, 64 * (p // 2 % 2) + 32 * (p // 4)
            total = (part[e, x, b, r0:r0 + 32, :w] + rxb[e, b, r0:r0 + 32, :w].astype(F32)
                     + rxc[e, b, r0:r0 + 32, :w].astype(F32))
            zs[e, p, :, :w] = total.astype(BF16)
        for dz in (4, 3, 5, 2, 6, 1, 7, 0):
            to = (z + dz) % NZ
            send(zs.at[e, to, :, pl.ds(0, w)], zr.at[e, z, :, pl.ds(0, w)], zsem.at[e],
                 cidx(to, x, kk), origins[e], zgsem)

    mine = kk == z // 2 % 2
    slot = 2 * kk + z // 4

    def finish(e, total):
        w = cols[e]
        lo = 128 if e == 4 else 0
        fs[e, :, :w] = total * wscale
        to = cidx(2 * senders[e] + z % 2, x, z // 2 % 2)
        local = mine & (senders[e] == z // 2)
        remote = jnp.logical_not(local)
        pending.append((remote, send(fs.at[e, :, pl.ds(0, w)], fr.at[slot, :, pl.ds(lo, w)], fsem, to, h,
                                     group(), remote)))

        @pl.when(local)
        def _():
            fr[slot, :, lo:lo + w] = fs[e, :, :w]

    def zdone(e):
        w = cols[e]
        arrived(zr.at[e, :, :, pl.ds(0, w)], zsem.at[e])
        total = zr[e, 0, :, :w].astype(F32)
        for zz in range(1, NZ):
            total = total + zr[e, zz, :, :w].astype(F32)
        finish(e, total)

    def zfirst(e):
        for p in range(NZ):
            b, r0 = p % 2, 64 * (p // 2 % 2) + 32 * (p // 4)
            zfs[e, p] = part[e, :, b, r0:r0 + 32, :].astype(BF16)
        for dz in range(1, NZ):
            to = (z + dz) % NZ
            send(zfs.at[e, to], zfr.at[e, z], zsem.at[e], cidx(to, x, kk), h, zfsem[e])
        zfr[e, z] = zfs[e, z]
        sent(zfr.at[e, pl.ds(0, 7)], zfsem[e])

    def xnext(e):
        arrived(zfr.at[e, pl.ds(0, 7)], zsem.at[e])
        for xx in range(NX):
            total = zfr[e, 0, xx].astype(F32)
            for zz in range(1, NZ):
                total = total + zfr[e, zz, xx].astype(F32)
            xfs[e, xx] = total.astype(BF16)
        for dx in (2, 1, 3) if e == 0 else (2, 1, 3, 0):
            to = (x + dx) % NX
            send(xfs.at[e, to], xfr.at[e, x], xsem.at[0, e], cidx(z, to, kk), origins[e], xfsem[e])
        if e == 0:
            xfr[e, x] = xfs[e, x]
            sent(xfr.at[e, pl.ds(0, 3)], xfsem[e])
        else:
            sent(xfr.at[e], xfsem[e])

    def xlast(e):
        arrived(xfr.at[e, pl.ds(0, 3)] if e == 0 else xfr.at[e], xsem.at[0, e])
        total = xfr[e, 0].astype(F32)
        for xx in range(1, NX):
            total = total + xfr[e, xx].astype(F32)
        finish(e, total)

    def key_step(j, carry):
        at = pl.ds(pl.multiple_of(128 * j, 128), 128)
        ks[:, at] = (factor * (kloc[j] + mm(vh[j], later[j], NT))).astype(BF16)
        return carry

    def query_step(j, carry):
        at = pl.ds(pl.multiple_of(128 * j, 128), 128)
        qs[:, at] = (factor * (qloc[j] + mm(gh[j], prior[j], NT))).astype(BF16)
        return carry

    def put(src, dst, n):
        pltpu.make_async_copy(src, dst, osem.at[n]).start()

    xo = (x + 2) % NX

    def wblock(u, b, at):
        return wbuf.at[(h + u) % NY, b, at, kk]

    wxsem, wrsem, wssem = group(), group(), group()

    def wx(u):
        for b in range(2):
            send(wblock(u, b, x), wblock(u, b, x), w3sem.at[2 * b, u], cidx(z, xr, kk), h, wxsem)
            send(wblock(u, 1 - b, x), wblock(u, 1 - b, x), w3sem.at[1 + b, u], cidx(z, xl, kk), h, wxsem)

    def wrelay(u):
        arrived(wblock(u, 0, xl), w3sem.at[0, u])
        send(wblock(u, 0, xl), wblock(u, 0, xl), w3sem.at[3, u], cidx(z, xr, kk), h, wrsem)
        arrived(wblock(u, 1, xr), w3sem.at[1, u])
        send(wblock(u, 1, xr), wblock(u, 1, xr), w3sem.at[3, u], cidx(z, xl, kk), h, wrsem)

    def wsib(u, n):
        ref = wbuf.at[(h + u) % NY, :, (x, xl, xr, xo)[n], kk]
        send(ref, ref, w4sem.at[u], sib, h, wssem)

    def wneighbours(u):
        arrived(wbuf.at[(h + u) % NY, :, xl, kk], w3sem.at[2, u])
        wsib(u, 1)
        wsib(u, 2)

    def wopposite(u):
        arrived(wbuf.at[(h + u) % NY, :, xo, kk], w3sem.at[3, u])
        wsib(u, 3)

    def input_part(u):
        o = (h + u) % NY
        arrived(wbuf.at[o, :, :, 1 - kk], w4sem.at[u])

        def step(i, carry):
            b, x0 = i // 2, 2 * (i % 2)
            w = wbuf[o, b, pl.ds(x0, 2)].reshape(256, 512)
            p = mm(pair(vgall, o, 0, 2), w[:, :256], NT) + mm(pair(vgall, o, 2, 2), w[:, 256:], NT)
            if u == 3:
                ist[i] = (acc[i] + p).astype(BF16)
            else:
                acc[i] = p if u == 0 else acc[i] + p
            return carry
        lax.fori_loop(0, 4, step, 0)

    partial(0)
    zfirst(0)
    arrived(wz.at[pl.ds(0, 6)], w2sem)
    for u in range(NY):
        wx(u)
    scan3(wsk, z2k, zak, o3k, prior, 1, False)
    for u in range(NY):
        wsib(u, 0)
    transposed_part(vh, gh, qh, kloc)
    lax.fori_loop(0, 4, key_step, 0)
    put(ks, k_out, 0)

    for j in range(2):
        arrived(vgall.at[yl, j], ysem.at[0, j])
        send(vgall.at[yl, j], vgall.at[yl, j], ysem.at[2, j], c, yr, yrsem)
        arrived(vgall.at[yr, 2 + j], ysem.at[1, 2 + j])
        send(vgall.at[yr, 2 + j], vgall.at[yr, 2 + j], ysem.at[2, 2 + j], c, yl, yrsem)
    forward(1)
    partial(1)
    zfirst(1)
    wrelay(0)
    wrelay(1)
    straight_part(gh, vh, kh, qloc)

    for j in range(2):
        arrived(vgall.at[yl, 2 + j], ysem.at[0, 2 + j])
        arrived(vgall.at[yr, j], ysem.at[1, j])
    forward(2)
    partial(2)
    xsend1(2)

    for j in (0, 2):
        arrived(vgall.at[yo, j], ysem.at[2, j])
    forward(3)
    partial(3)
    xsend1(3)
    for j in (1, 3):
        arrived(vgall.at[yo, j], ysem.at[2, j])
    forward(4)
    partial(4)
    xsend1(4)
    xsend2(2)
    xnext(0)
    xsend2(3)
    scan_done(o3k, 1)
    lax.fori_loop(0, 4, query_step, 0)
    put(qs, q_out, 0)
    for u in range(2):
        wneighbours(u)
        wopposite(u)
    xsend2(4)
    input_part(0)
    xdone(2)
    xdone(3)
    xlast(0)
    xnext(1)
    wrelay(2)
    wrelay(3)
    xdone(4)
    input_part(1)
    wneighbours(2)
    wneighbours(3)
    xlast(1)
    wopposite(2)
    wopposite(3)
    zdone(2)
    input_part(2)
    zdone(3)
    zdone(4)
    input_part(3)
    for i in range(4):
        put(ist.at[i], i_out.at[:, pl.ds(256 * i, 256)], 1)
    sent(vgall.at[pl.ds(0, 2)], wxsem)
    sent(vgall.at[0], wrsem)
    sent(vgall, wssem)
    sent(vsib.at[pl.ds(0, 3)], xgsem)
    sent(zs.at[pl.ds(0, 2)], zgsem)

    @pl.when(mine)
    def _():
        arrived(fr.at[pl.ds(0, 3)], fsem)

    @pl.when(jnp.logical_not(mine))
    def _():
        arrived(fr, fsem)

    for n in range(4):
        put(fr.at[n], w_out.at[pl.ds(32 * (n % 2), 32), pl.ds(256 * (n // 2), 256)], 2)
    arrived(vgall.at[pl.ds(0, 2)], osem.at[0])
    arrived(ist, osem.at[1])
    arrived(fr, osem.at[2])
    for cond, desc in pending:
        if cond is None:
            desc.wait()
        else:
            pl.when(cond)(desc.wait_send)


def write_out(q_in, k_in, i_in, w_in, q_out, k_out, i_out, w_out, sems):
    pairs = [(src.at[pl.ds(at, 128)], dst.at[pl.ds(at, 128)])
             for at in range(0, 512, 128) for src, dst in ((i_in, i_out), (q_in, q_out), (k_in, k_out))]
    pairs.append((w_in, w_out))
    copies = [pltpu.make_async_copy(src, dst, sems.at[n]) for n, (src, dst) in enumerate(pairs)]
    for copy in copies:
        copy.start()
    for copy in copies:
        copy.wait()


def local(queries, keys, values, out_grad, inputs, value_weight):
    length = queries.shape[0]
    tokens = length * lax.axis_size("ctx")
    factor = 1.0 / math.sqrt(DH * tokens)
    wscale = 1.0 / math.sqrt(tokens)
    vm = pltpu.VMEM
    dma = pltpu.SemaphoreType.DMA
    scratch = [
        vm((4, 512, 128), BF16), vm((4, 512, 128), BF16), vm((4, 512, 128), BF16), vm((4, 512, 128), BF16),
        vm((2, 512, 1024), BF16), vm((2, 1024, 512), BF16),
        vm((8, 64, 512), BF16), vm((4, 2, 4, 2, 64, 512), BF16),
        vm((4, 128, 128), F32), vm((4, 128, 128), F32),
        vm((8, 64, 128), F32), vm((8, 64, 128), F32),
        vm((8, 64, 128), F32), vm((8, 64, 128), F32),
        vm((64, 128), BF16), vm((64, 128), BF16),
        vm((8, 64, 128), BF16), vm((8, 64, 128), BF16),
        vm((64, 128), F32), vm((64, 128), F32),
        vm((8, 64, 128), BF16), vm((8, 64, 128), BF16),
        vm((4, 128, 128), BF16), vm((4, 128, 128), BF16),
        vm((4, 512, 128), F32), vm((4, 512, 128), F32), vm((4, 512, 128), F32),
        vm((4, 4, 512, 128), BF16), vm((5, 2, 512, 128), BF16),
        vm((5, 4, 2, 128, 256), F32), vm((4, 512, 256), F32),
        vm((5, 2, 128, 256), BF16), vm((5, 2, 128, 256), BF16), vm((5, 2, 128, 256), BF16),
        vm((5, 2, 128, 256), BF16), vm((5, 2, 128, 256), BF16), vm((5, 2, 128, 256), BF16),
        vm((5, 8, 32, 256), BF16), vm((5, 8, 32, 256), BF16),
        vm((2, 8, 4, 32, 256), BF16), vm((2, 8, 4, 32, 256), BF16), vm((2, 4, 32, 256), BF16), vm((2, 4, 32, 256), BF16),
        vm((5, 32, 256), F32), vm((4, 32, 256), F32),
        vm((512, 512), BF16), vm((512, 512), BF16), vm((4, 512, 256), BF16),
        dma((6,)), dma((40,)), dma((2,)), dma((2, 8)), dma((2,)),
        dma((2, 5)), dma(()), dma((4, 4)), dma((4,)), dma(()), dma((3, 4)), dma((5,)), dma((3, 5)),
        dma((5,)), dma(()), dma((3,)),
    ]
    out_shape = (
        pltpu.VMEM((512, 512), BF16),
        pltpu.VMEM((512, 512), BF16),
        pltpu.VMEM((512, 1024), BF16),
        pltpu.VMEM((64, 512), F32),
    )
    results = pl.pallas_call(
        functools.partial(kernel, factor, wscale),
        out_shape=out_shape,
        in_specs=[pl.BlockSpec(memory_space=pl.ANY)] * 6,
        out_specs=[pl.BlockSpec(memory_space=pl.ANY)] * 4,
        scratch_shapes=scratch,
        compiler_params=pltpu.CompilerParams(
            collective_id=0, has_side_effects=True, vmem_limit_bytes=56 * 1024 * 1024),
        name="attention_backward",
    )(queries, keys, values, out_grad, inputs, value_weight)
    return pl.pallas_call(
        write_out,
        out_shape=tuple(jax.ShapeDtypeStruct(r.shape, r.dtype) for r in results),
        in_specs=[pl.BlockSpec(memory_space=pltpu.VMEM)] * 4,
        out_specs=[pl.BlockSpec(memory_space=pl.ANY)] * 4,
        scratch_shapes=[dma((13,))],
        name="write_out",
    )(*(pltpu.with_memory_space_constraint(r, pltpu.VMEM) for r in results))


def solution(mesh):
    spec = P("ctx", "head")
    return jax.shard_map(
        local, mesh=mesh, in_specs=(spec,) * 6, out_specs=(spec,) * 4, check_vma=False)
```
